128 devices in a mesh: sec: 64 (over y, x_lo, z, core), scan: 2 (over x_hi).
Axes of the slice: x: 4 (x_hi: 2, x_lo: 2; x = x_hi * 2 + x_lo), y: 4, z: 4, core: 2. Of those that a mesh axis runs over, the one named last changes fastest.
Arguments:
- obj_amp: float32 [64, 512, 512], P('sec', 'scan'), may hold values from 0.97 to 1
- obj_phase: float32 [64, 512, 512], P('sec', 'scan'), may hold values from -3.140625 to 3.140625
- forward_waves: bfloat16 [64, 16, 2, 256, 256], P('sec', 'scan'), may hold values from -6 to 6
- exit_adjoint: bfloat16 [16, 2, 256, 256], P('scan'), may hold values from -6 to 6
- offsets: int32 [16, 2], P('scan'), may hold values from 0 to 256
Outputs:
- object_grad: float32 [64, 2, 512, 512], P('sec', None, 'scan')
The draws below stay inside these ranges and needn't reach their ends.
All inputs are finite; a program needn't handle non-finite values.
Results may differ from the reference program's by a relative error of at most 0.012.
The reference program's roundings to bfloat16 on the way count: a program that leaves them out, or rounds other values in their place, can miss the bound.
Values may be sent and summed in bfloat16 or wider, within the bound.
A program may use at most 64 MiB of HBM per device.

```python
import jax
import jax.numpy as jnp
from jax import lax

W = 256
OBJ = 512
SUBSTEPS = 2
POS = 16
NSL = 64


def set_ends(entries, rng, least, largest):
    index_at = [jax.random.randint(jax.random.fold_in(rng, axis), (), 0, length) for axis, length in enumerate(entries.shape)]
    widest = entries.shape.index(max(entries.shape))
    neighbour = index_at[:widest] + [(index_at[widest] + 1) % entries.shape[widest]] + index_at[widest + 1:]
    return entries.at[tuple(index_at)].set(least).at[tuple(neighbour)].set(largest)


def block_scale(rng, dims, pieces, least, largest):
    gain = 1.0
    for dim, shards_of in pieces:
        steps = jax.random.uniform(jax.random.fold_in(jax.random.fold_in(rng, 6), dim), (shards_of,), jnp.float32, least / len(pieces), largest / len(pieces))
        gain = gain * jnp.repeat(jnp.exp(steps), dims[dim] // shards_of).reshape((-1,) + (1,) * (len(dims) - 1 - dim))
    return gain


def noise(rng, shape, width, bound, pieces=(), held_as=jnp.bfloat16):
    drawn = jax.random.normal(rng, shape, jnp.float32) * width
    if len(pieces) > 0:
        drawn = block_scale(rng, shape, pieces, -0.22, 0.18) * drawn
    return jnp.clip(drawn, min=-bound, max=bound).astype(held_as)


def setup_inputs(seed: int = 0) -> dict:
    keys = jax.random.split(jax.random.key(seed), 6)
    return {
        "obj_amp": jnp.clip(0.97 + 0.029999971 * jax.random.uniform(keys[0], (NSL, OBJ, OBJ), jnp.float32) ** block_scale(keys[0], (NSL, OBJ, OBJ), ((0, 64), (1, 2)), -0.2, 0.2), 0.97, 1.0),
        "obj_phase": jnp.clip(jax.random.uniform(keys[1], (NSL, OBJ, OBJ), jnp.float32, -3.140625, 3.140625), -3.140625, 3.140625),
        "forward_waves": noise(keys[2], (NSL, POS, 2, W, W), 1.0, 6.0, ((0, 64), (1, 2))),
        "exit_adjoint": noise(keys[3], (POS, 2, W, W), 1.0, 6.0, ((0, 2),)),
        "offsets": set_ends(jax.random.randint(keys[4], (POS, 2), 0, OBJ - W + 1), jax.random.fold_in(keys[4], 1), 0, OBJ - W).astype(jnp.int32),
    }


damping = 0.0005
turning = 0.011


def laplacian(field):
    widths = [(0, 0)] * (field.ndim - 2) + [(1, 1), (1, 1)]
    padded = jnp.pad(field, widths)
    beside = padded[..., 2:, 1:-1] + padded[..., :-2, 1:-1] + padded[..., 1:-1, 2:] + padded[..., 1:-1, :-2]
    return beside - 4.0 * field


def back_step(field):
    for substep in range(SUBSTEPS):
        lap_re = laplacian(field[..., 0, :, :])
        lap_im = laplacian(field[..., 1, :, :])
        new_re = field[..., 0, :, :] + damping * lap_re + turning * lap_im
        new_im = field[..., 1, :, :] + damping * lap_im - turning * lap_re
        field = jnp.stack([new_re, new_im], axis=-3)
    return field


def reference(obj_amp, obj_phase, forward_waves, exit_adjoint, offsets):
    trans_re = obj_amp * jnp.cos(obj_phase)
    trans_im = obj_amp * jnp.sin(obj_phase)
    gradient = jnp.zeros((NSL, 2, OBJ, OBJ), jnp.float32)

    def per_position(gradient, position):
        row_at = offsets[position, 0].astype(jnp.int32)
        col_at = offsets[position, 1].astype(jnp.int32)
        adjoint = exit_adjoint[position].astype(jnp.float32)

        def per_slice(carry, layer):
            gradient, adjoint = carry
            spread = back_step(adjoint)
            incoming = forward_waves[layer, position].astype(jnp.float32)
            part_re = incoming[0] * spread[0] + incoming[1] * spread[1]
            part_im = incoming[0] * spread[1] - incoming[1] * spread[0]
            zero_index = jnp.zeros((), jnp.int32)
            current = lax.dynamic_slice(gradient, (layer, zero_index, row_at, col_at), (1, 2, W, W))
            added = current + jnp.stack([part_re, part_im])[None]
            gradient = lax.dynamic_update_slice(gradient, added, (layer, zero_index, row_at, col_at))
            win_re = lax.dynamic_slice(trans_re, (layer, row_at, col_at), (1, W, W))[0]
            win_im = lax.dynamic_slice(trans_im, (layer, row_at, col_at), (1, W, W))[0]
            out_re = win_re * spread[0] + win_im * spread[1]
            out_im = win_re * spread[1] - win_im * spread[0]
            leaving = jnp.stack([out_re, out_im]).astype(jnp.bfloat16)
            adjoint = lax.optimization_barrier(leaving).astype(jnp.float32)
            return (gradient, adjoint), None

        layers = jnp.arange(NSL, dtype=jnp.int32)
        (gradient, adjoint), unused = lax.scan(per_slice, (gradient, adjoint), layers, reverse=True)
        return gradient, None

    gradient, unused = lax.scan(per_position, gradient, jnp.arange(POS, dtype=jnp.int32))
    return gradient
```

```python
import functools

import jax
import jax.numpy as jnp
from jax import lax
from jax.experimental import pallas as pl
from jax.experimental.pallas import tpu as pltpu
from jax.sharding import PartitionSpec as P

MESH = pl.DeviceIdType.MESH

damping = 0.0005
turning = 0.011

G = 8
R = 16
SKEW = 2 * G
W = 256
OBJ = 512
S = (W + SKEW) // R
TOP = 16
ROWS = OBJ + 40
COLS = OBJ + 128
FIX = 32767.0
HELD = jnp.int16


def extract_kernel(offs_ref, trans_ref, win_ref, padded):
    order = G - 1 - lax.rem(lax.axis_index("sec"), G)
    delay = 2 * (order + 1)
    padded[...] = jnp.zeros_like(padded)
    padded[:, TOP : TOP + OBJ, 0:OBJ] = trans_ref[...]

    def per_strip(strip, unused):
        at = lax.broadcasted_iota(jnp.int32, (R, W), 0) + (strip * R - delay)
        inside = jnp.logical_and(at >= 0, at < W)
        for position in range(G):
            row_at = offs_ref[position, 0]
            col_at = offs_ref[position, 1]
            base = pl.multiple_of(col_at // 128 * 128, 128)
            turn = lax.rem(384 - lax.rem(col_at, 128), 384)
            top_row = row_at + (strip * R - delay + TOP)
            row_base = pl.multiple_of(top_row // 8 * 8, 8)
            row_turn = lax.rem(R + 8 - lax.rem(top_row, 8), R + 8)
            for part in range(2):
                rows = padded[part, pl.ds(row_base, R + 8), pl.ds(base, 384)]
                rows = pltpu.roll(rows, row_turn, 0)[0:R]
                rows = pltpu.roll(rows, turn, 1)[:, 0:W]
                rows = jnp.where(inside, rows, 0.0) * FIX
                rows = jnp.where(rows >= 0.0, rows + 0.5, rows - 0.5)
                win_ref[position, strip, part] = rows.astype(jnp.int32).astype(HELD)
        return unused

    lax.fori_loop(0, S, per_strip, 0)


def extract(offsets, trans):
    return pl.pallas_call(
        extract_kernel,
        out_shape=jax.ShapeDtypeStruct((G, S, 2, R, W), HELD),
        in_specs=[
            pl.BlockSpec(memory_space=pltpu.SMEM),
            pl.BlockSpec(memory_space=pltpu.VMEM),
        ],
        out_specs=pl.BlockSpec(memory_space=pltpu.VMEM),
        scratch_shapes=[pltpu.VMEM((2, ROWS, COLS), jnp.float32)],
        name="extract",
    )(offsets, trans)


def laplace(low, mid, high, first, last):
    left = jnp.where(first, 0.0, pltpu.roll(mid, 1, 1))
    right = jnp.where(last, 0.0, pltpu.roll(mid, W - 1, 1))
    return (low + high) + (left + right) - 4.0 * mid


def substep(buf, order, first, last):
    mid_re = buf[order, 0, 7 : 7 + R, :]
    mid_im = buf[order, 1, 7 : 7 + R, :]
    lap_re = laplace(buf[order, 0, 6 : 6 + R, :], mid_re, buf[order, 0, 8 : 8 + R, :], first, last)
    lap_im = laplace(buf[order, 1, 6 : 6 + R, :], mid_im, buf[order, 1, 8 : 8 + R, :], first, last)
    new_re = mid_re + damping * lap_re + turning * lap_im
    new_im = mid_im + damping * lap_im - turning * lap_re
    return new_re, new_im


def sweep_kernel(
    win_ref, exit_ref, spr_ref, trans, inbox, spread_out, wave_out, waves, halves,
    trans_sem, in_sem, spr_sem, trans_sent, spr_sent, wave_sent,
):
    sec = lax.axis_index("sec")
    scan = lax.axis_index("scan")
    group = sec // G
    member = lax.rem(sec, G)
    groups = lax.axis_size("sec") // G
    top = group == groups - 1

    def at(g, m):
        return (g * G + m, scan)

    barrier = pltpu.get_barrier_semaphore()
    for step in range(1, G):
        pl.semaphore_signal(barrier, 1, device_id=at(group, lax.rem(member + step, G)), device_id_type=MESH)

    @pl.when(group > 0)
    def _():
        pl.semaphore_signal(barrier, 1, device_id=at(group - 1, member), device_id_type=MESH)

    @pl.when(jnp.logical_not(top))
    def _():
        pl.semaphore_signal(barrier, 1, device_id=at(group + 1, member), device_id_type=MESH)

    waves[...] = jnp.zeros_like(waves)
    halves[...] = jnp.zeros_like(halves)
    inbox[S - 1] = jnp.zeros((2, R, W), jnp.bfloat16)
    pl.semaphore_wait(barrier, G - 1 + jnp.where(group > 0, 1, 0) + jnp.where(top, 0, 1))

    def give(strip, unused):
        pltpu.make_async_copy(
            win_ref.at[member, strip], trans.at[strip, G - 1 - member], trans_sem.at[strip]
        ).start()
        for step in range(1, G):
            other = lax.rem(member + step, G)
            pltpu.make_async_remote_copy(
                src_ref=win_ref.at[other, strip],
                dst_ref=trans.at[strip, G - 1 - member],
                send_sem=trans_sent,
                recv_sem=trans_sem.at[strip],
                device_id=at(group, other),
                device_id_type=MESH,
            ).start()
        return unused

    lax.fori_loop(0, S, give, 0)

    @pl.when(top)
    def _():
        def feed(strip, unused):
            pltpu.make_async_copy(exit_ref.at[strip], inbox.at[strip], in_sem.at[strip]).start()
            return unused

        lax.fori_loop(0, S - 1, feed, 0)

    lane = lax.broadcasted_iota(jnp.int32, (R, W), 1)
    first = lane == 0
    last = lane == W - 1
    row = lax.broadcasted_iota(jnp.int32, (R, W), 0)

    def one_strip(strip, unused):
        @pl.when(strip < S - 1)
        def _():
            pltpu.make_async_copy(inbox.at[strip], inbox.at[strip], in_sem.at[strip]).wait()

        pltpu.make_async_copy(trans.at[strip], trans.at[strip], trans_sem.at[strip]).wait()
        wave_re = inbox[strip, 0].astype(jnp.float32)
        wave_im = inbox[strip, 1].astype(jnp.float32)
        for order in range(G):
            waves[order, 0, 8 : 8 + R, :] = wave_re
            waves[order, 1, 8 : 8 + R, :] = wave_im
            half_re, half_im = substep(waves, order, first, last)
            at_row = row + (strip * R - 2 * order - 1)
            inside = jnp.logical_and(at_row >= 0, at_row < W)
            halves[order, 0, 8 : 8 + R, :] = jnp.where(inside, half_re, 0.0)
            halves[order, 1, 8 : 8 + R, :] = jnp.where(inside, half_im, 0.0)
            spread_re, spread_im = substep(halves, order, first, last)
            waves[order, :, 0:8, :] = waves[order, :, R : R + 8, :]
            halves[order, :, 0:8, :] = halves[order, :, R : R + 8, :]
            spread_out[strip, order, 0] = spread_re.astype(jnp.bfloat16)
            spread_out[strip, order, 1] = spread_im.astype(jnp.bfloat16)
            win_re = trans[strip, order, 0].astype(jnp.int32).astype(jnp.float32)
            win_im = trans[strip, order, 1].astype(jnp.int32).astype(jnp.float32)
            out_re = ((win_re * spread_re + win_im * spread_im) * (1.0 / FIX)).astype(jnp.bfloat16)
            out_im = ((win_re * spread_im - win_im * spread_re) * (1.0 / FIX)).astype(jnp.bfloat16)
            owner = G - 1 - order

            @pl.when(owner == member)
            def _():
                pltpu.make_async_copy(
                    spread_out.at[strip, order], spr_ref.at[member, strip], spr_sem
                ).start()

            @pl.when(owner != member)
            def _():
                pltpu.make_async_remote_copy(
                    src_ref=spread_out.at[strip, order],
                    dst_ref=spr_ref.at[member, strip],
                    send_sem=spr_sent,
                    recv_sem=spr_sem,
                    device_id=at(group, owner),
                    device_id_type=MESH,
                ).start()

            if order < G - 1:
                wave_re = out_re.astype(jnp.float32)
                wave_im = out_im.astype(jnp.float32)
            else:
                wave_out[strip, 0] = out_re
                wave_out[strip, 1] = out_im

        @pl.when(jnp.logical_and(strip > 0, group > 0))
        def _():
            pltpu.make_async_remote_copy(
                src_ref=wave_out.at[strip],
                dst_ref=inbox.at[strip - 1],
                send_sem=wave_sent,
                recv_sem=in_sem.at[strip - 1],
                device_id=at(group - 1, member),
                device_id_type=MESH,
            ).start()

        return unused

    lax.fori_loop(0, S, one_strip, 0)
    pltpu.make_async_copy(win_ref.at[0 : G - 1], win_ref.at[0 : G - 1], trans_sent).wait()
    pltpu.make_async_copy(spr_ref.at[0 : G - 1], spr_ref.at[0 : G - 1], spr_sent).wait()

    @pl.when(group > 0)
    def _():
        pltpu.make_async_copy(wave_out.at[0 : S - 1], wave_out.at[0 : S - 1], wave_sent).wait()

    pltpu.make_async_copy(spr_ref, spr_ref, spr_sem).wait()


def sweep(win, exit_wave):
    return pl.pallas_call(
        sweep_kernel,
        out_shape=jax.ShapeDtypeStruct((G, S, 2, R, W), jnp.bfloat16),
        in_specs=[pl.BlockSpec(memory_space=pltpu.VMEM)] * 2,
        out_specs=pl.BlockSpec(memory_space=pltpu.VMEM),
        scratch_shapes=[
            pltpu.VMEM((S, G, 2, R, W), HELD),
            pltpu.VMEM((S, 2, R, W), jnp.bfloat16),
            pltpu.VMEM((S, G, 2, R, W), jnp.bfloat16),
            pltpu.VMEM((S, 2, R, W), jnp.bfloat16),
            pltpu.VMEM((G, 2, R + 8, W), jnp.float32),
            pltpu.VMEM((G, 2, R + 8, W), jnp.float32),
            pltpu.SemaphoreType.DMA((S,)),
            pltpu.SemaphoreType.DMA((S,)),
            pltpu.SemaphoreType.DMA,
            pltpu.SemaphoreType.DMA,
            pltpu.SemaphoreType.DMA,
            pltpu.SemaphoreType.DMA,
        ],
        compiler_params=pltpu.CompilerParams(collective_id=0, has_side_effects=True),
        name="sweep",
    )(win, exit_wave)


def gather_kernel(offs_ref, waves_ref, spr_ref, grad_ref, acc):
    order = G - 1 - lax.rem(lax.axis_index("sec"), G)
    delay = 2 * (order + 1)
    acc[...] = jnp.zeros_like(acc)

    for position in range(G):
        row_at = offs_ref[position, 0]
        col_at = offs_ref[position, 1]
        base = pl.multiple_of(col_at // 128 * 128, 128)
        turn = lax.rem(col_at, 128)

        def per_strip(strip, unused):
            fwd_re = waves_ref[position, strip, 0].astype(jnp.float32)
            fwd_im = waves_ref[position, strip, 1].astype(jnp.float32)
            spread_re = spr_ref[position, strip, 0].astype(jnp.float32)
            spread_im = spr_ref[position, strip, 1].astype(jnp.float32)
            at = lax.broadcasted_iota(jnp.int32, (R, W), 0) + (strip * R - delay)
            inside = jnp.logical_and(at >= 0, at < W)
            part_re = jnp.where(inside, fwd_re * spread_re + fwd_im * spread_im, 0.0)
            part_im = jnp.where(inside, fwd_re * spread_im - fwd_im * spread_re, 0.0)
            beside = jnp.zeros((R, 128), jnp.float32)
            below = jnp.zeros((8, 384), jnp.float32)
            top_row = row_at + (strip * R - delay + TOP)
            rows = pl.ds(pl.multiple_of(top_row // 8 * 8, 8), R + 8)
            row_turn = lax.rem(top_row, 8)
            for part, value in enumerate((part_re, part_im)):
                wide = pltpu.roll(jnp.concatenate([value, beside], axis=1), turn, 1)
                tall = pltpu.roll(jnp.concatenate([wide, below], axis=0), row_turn, 0)
                acc[part, rows, pl.ds(base, 384)] += tall
            return unused

        lax.fori_loop(0, S, per_strip, 0)

    grad_ref[...] = acc[:, TOP : TOP + OBJ, 0:OBJ]


def gather(offsets, waves, spread):
    return pl.pallas_call(
        gather_kernel,
        out_shape=jax.ShapeDtypeStruct((2, OBJ, OBJ), jnp.float32),
        in_specs=[
            pl.BlockSpec(memory_space=pltpu.SMEM),
            pl.BlockSpec(memory_space=pltpu.VMEM),
            pl.BlockSpec(memory_space=pltpu.VMEM),
        ],
        out_specs=pl.BlockSpec(memory_space=pltpu.VMEM),
        scratch_shapes=[pltpu.VMEM((2, ROWS, COLS), jnp.float32)],
        name="gather",
    )(offsets, waves, spread)


def on_device(obj_amp, obj_phase, forward_waves, exit_adjoint, offsets):
    trans = jnp.concatenate([obj_amp * jnp.cos(obj_phase), obj_amp * jnp.sin(obj_phase)])
    trans = lax.all_gather(trans, "scan", axis=1, tiled=True)
    win = extract(offsets, trans)
    member = lax.rem(lax.axis_index("sec"), G)
    own = lax.dynamic_index_in_dim(exit_adjoint, member, 0, keepdims=False)
    own = jnp.transpose(own.reshape(2, W // R, R, W), (1, 0, 2, 3))
    spread = sweep(win, own)
    delay = 2 * (G - member)
    waves = jnp.pad(forward_waves[0], ((0, 0), (0, 0), (SKEW, SKEW), (0, 0)))
    waves = lax.dynamic_slice_in_dim(waves, SKEW - delay, W + SKEW, 2)
    waves = jnp.transpose(waves.reshape(G, 2, S, R, W), (0, 2, 1, 3, 4))
    gradient = gather(offsets, waves, spread)
    reduced = lax.psum_scatter(gradient, "scan", scatter_dimension=1, tiled=True)
    return reduced[None]


def solution(mesh):
    in_specs = (
        P("sec", "scan", None),
        P("sec", "scan", None),
        P("sec", "scan", None, None, None),
        P("scan", None, None, None),
        P("scan", None),
    )
    out_specs = P("sec", None, "scan", None)
    return jax.shard_map(
        on_device, mesh=mesh, in_specs=in_specs, out_specs=out_specs, check_vma=False
    )
```

```python
import functools

import jax
import jax.numpy as jnp
from jax import lax
from jax.experimental import pallas as pl
from jax.experimental.pallas import tpu as pltpu
from jax.sharding import PartitionSpec as P

MESH = pl.DeviceIdType.MESH

damping = 0.0005
turning = 0.011

G = 8
R = 16
SKEW = 2 * G
W = 256
OBJ = 512
S = (W + SKEW) // R
TOP = 16
ROWS = OBJ + 40
LATE = 5
COLS = OBJ + 128
FIX = 32767.0
HELD = jnp.int16
BLOCK = 32
BLOCKS = OBJ // 2 // BLOCK


def swap_kernel(half_ref, other_ref, sent, come):
    partner = (lax.axis_index("sec"), 1 - lax.axis_index("scan"))
    barrier = pltpu.get_barrier_semaphore()
    pl.semaphore_signal(barrier, 1, device_id=partner, device_id_type=MESH)
    pl.semaphore_wait(barrier, 1)
    copy = pltpu.make_async_remote_copy(
        src_ref=half_ref, dst_ref=other_ref, send_sem=sent, recv_sem=come, device_id=partner, device_id_type=MESH
    )
    copy.start()
    copy.wait()


def swap(half):
    return pl.pallas_call(
        swap_kernel,
        out_shape=jax.ShapeDtypeStruct(half.shape, half.dtype),
        in_specs=[pl.BlockSpec(memory_space=pltpu.VMEM)],
        out_specs=pl.BlockSpec(memory_space=pltpu.VMEM),
        scratch_shapes=[pltpu.SemaphoreType.DMA, pltpu.SemaphoreType.DMA],
        compiler_params=pltpu.CompilerParams(collective_id=1, has_side_effects=True),
        name="swap",
    )(half)


def turned(pieces, amount, axis, before):
    length = pieces[0].shape[axis]
    places = lax.broadcasted_iota(jnp.int32, pieces[0].shape, axis)
    if before:
        keep = places < length - amount
        rolled = [pltpu.roll(piece, lax.rem(length - amount, length), axis) for piece in pieces]
        return [jnp.where(keep, rolled[i], rolled[i + 1]) for i in range(len(pieces) - 1)]
    keep = places >= amount
    rolled = [pltpu.roll(piece, amount, axis) for piece in pieces]
    zero = jnp.zeros_like(pieces[0])
    rolled = [zero] + rolled + [zero]
    return [jnp.where(keep, rolled[i + 1], rolled[i]) for i in range(len(pieces) + 1)]


def extract_kernel(offs_ref, half_ref, other_ref, win_ref, padded):
    scan = lax.axis_index("scan")
    order = G - 1 - lax.rem(lax.axis_index("sec"), G)
    delay = 2 * (order + 1)
    padded[:, 0:TOP, :] = jnp.zeros((2, TOP, COLS), jnp.int32)
    padded[:, TOP + OBJ :, :] = jnp.zeros((2, ROWS - TOP - OBJ, COLS), jnp.int32)
    padded[:, :, OBJ:] = jnp.zeros((2, ROWS, COLS - OBJ), jnp.int32)

    def place(source, start):
        def some_rows(block, unused):
            rows = pl.ds(pl.multiple_of(block * 32, 32), 32)
            to = pl.ds(pl.multiple_of(start + block * 32, 8), 32)
            for part in range(2):
                padded[part, to, 0:OBJ] = source[part, rows, :].astype(jnp.int32)
            return unused

        lax.fori_loop(0, OBJ // 64, some_rows, 0)

    place(half_ref, pl.multiple_of(TOP + scan * (OBJ // 2), 8))
    place(other_ref, pl.multiple_of(TOP + (1 - scan) * (OBJ // 2), 8))

    def per_strip(strip, unused):
        at = lax.broadcasted_iota(jnp.int32, (R, 128), 0) + (strip * R - delay)
        inside = jnp.logical_and(at >= 0, at < W)
        for position in range(G):
            row_at = offs_ref[position, 0]
            col_at = offs_ref[position, 1]
            base = pl.multiple_of(col_at // 128 * 128, 128)
            top_row = row_at + (strip * R - delay + TOP)
            row_base = pl.multiple_of(top_row // 8 * 8, 8)
            for part in range(2):
                whole = padded[part, pl.ds(row_base, R + 8), pl.ds(base, 384)]
                tiles = [
                    turned([whole[8 * i : 8 * i + 8, 128 * j : 128 * j + 128] for j in range(3)], lax.rem(col_at, 128), 1, True)
                    for i in range(R // 8 + 1)
                ]
                for j in range(2):
                    column = turned([tile[j] for tile in tiles], lax.rem(top_row, 8), 0, True)
                    column = jnp.where(inside, jnp.concatenate(column, axis=0), 0)
                    win_ref[position, strip, part, :, 128 * j : 128 * j + 128] = column.astype(HELD)
        return unused

    lax.fori_loop(0, S, per_strip, 0)


def extract(offsets, half, other):
    return pl.pallas_call(
        extract_kernel,
        out_shape=jax.ShapeDtypeStruct((G, S, 2, R, W), HELD),
        in_specs=[
            pl.BlockSpec(memory_space=pltpu.SMEM),
            pl.BlockSpec(memory_space=pltpu.VMEM),
            pl.BlockSpec(memory_space=pltpu.VMEM),
        ],
        out_specs=pl.BlockSpec(memory_space=pltpu.VMEM),
        scratch_shapes=[pltpu.VMEM((2, ROWS, COLS), jnp.int32)],
        name="extract",
    )(offsets, half, other)


def laplace(low, mid, high, first, last):
    left = jnp.where(first, 0.0, pltpu.roll(mid, 1, 1))
    right = jnp.where(last, 0.0, pltpu.roll(mid, W - 1, 1))
    return (low + high) + (left + right) - 4.0 * mid


def substep(buf, order, first, last):
    mid_re = buf[order, 0, 7 : 7 + R, :]
    mid_im = buf[order, 1, 7 : 7 + R, :]
    lap_re = laplace(buf[order, 0, 6 : 6 + R, :], mid_re, buf[order, 0, 8 : 8 + R, :], first, last)
    lap_im = laplace(buf[order, 1, 6 : 6 + R, :], mid_im, buf[order, 1, 8 : 8 + R, :], first, last)
    new_re = mid_re + damping * lap_re + turning * lap_im
    new_im = mid_im + damping * lap_im - turning * lap_re
    return new_re, new_im


def sweep_kernel(
    windows, exit_ref, spr_ref, trans, inbox, spread_out, wave_out, waves, halves, tall,
    trans_sem, in_sem, spr_sem, trans_sent, spr_sent, wave_sent,
):
    sec = lax.axis_index("sec")
    scan = lax.axis_index("scan")
    group = sec // G
    member = lax.rem(sec, G)
    groups = lax.axis_size("sec") // G
    top = group == groups - 1

    def at(g, m):
        return (g * G + m, scan)

    barrier = pltpu.get_barrier_semaphore()
    for step in range(1, G):
        pl.semaphore_signal(barrier, 1, device_id=at(group, lax.rem(member + step, G)), device_id_type=MESH)

    @pl.when(group > 0)
    def _():
        pl.semaphore_signal(barrier, 1, device_id=at(group - 1, member), device_id_type=MESH)

    @pl.when(jnp.logical_not(top))
    def _():
        pl.semaphore_signal(barrier, 1, device_id=at(group + 1, member), device_id_type=MESH)

    pl.semaphore_wait(barrier, G - 1 + jnp.where(group > 0, 1, 0) + jnp.where(top, 0, 1))
    waves[...] = jnp.zeros_like(waves)
    halves[...] = jnp.zeros_like(halves)
    tall[...] = jnp.zeros_like(tall)
    inbox[S - 1] = jnp.zeros((2, R, W), jnp.bfloat16)
    @pl.when(top)
    def _():
        def feed(strip, unused):
            inbox[strip] = exit_ref[strip]
            return unused

        lax.fori_loop(0, S - 1, feed, 0)

    mine = G - 1 - member

    def give(strip, unused):
        for step in range(1, G):
            person = lax.rem(member + step, G)
            pltpu.make_async_remote_copy(
                src_ref=windows.at[person, strip],
                dst_ref=trans.at[strip, mine],
                send_sem=trans_sent,
                recv_sem=trans_sem.at[strip],
                device_id=at(group, person),
                device_id_type=MESH,
            ).start()
        return unused

    lax.fori_loop(0, S, give, 0)

    def own(strip, unused):
        trans[strip, mine] = windows[member, strip]
        return unused

    lax.fori_loop(0, S, own, 0)

    lane = lax.broadcasted_iota(jnp.int32, (R, W), 1)
    first = lane == 0
    last = lane == W - 1
    row = lax.broadcasted_iota(jnp.int32, (R, W), 0)

    def send_spread(strip, order):
        pltpu.make_async_remote_copy(
            src_ref=spread_out.at[strip, order],
            dst_ref=spr_ref.at[member, strip],
            send_sem=spr_sent,
            recv_sem=spr_sem,
            device_id=at(group, G - 1 - order),
            device_id_type=MESH,
        ).start()

    def one_strip(strip, unused):
        @pl.when(jnp.logical_and(strip < S - 1, jnp.logical_not(top)))
        def _():
            pltpu.make_async_copy(inbox.at[strip], inbox.at[strip], in_sem.at[strip]).wait()

        pltpu.make_async_copy(
            trans.at[strip, 0 : G - 1], trans.at[strip, 0 : G - 1], trans_sem.at[strip]
        ).wait()
        before = jnp.maximum(strip - 1, 0)
        wave_re = inbox[strip, 0].astype(jnp.float32)
        wave_im = inbox[strip, 1].astype(jnp.float32)
        for order in range(G):
            waves[order, 0, 8 : 8 + R, :] = wave_re
            waves[order, 1, 8 : 8 + R, :] = wave_im
            half_re, half_im = substep(waves, order, first, last)
            at_row = row + (strip * R - 2 * order - 1)
            inside = jnp.logical_and(at_row >= 0, at_row < W)
            halves[order, 0, 8 : 8 + R, :] = jnp.where(inside, half_re, 0.0)
            halves[order, 1, 8 : 8 + R, :] = jnp.where(inside, half_im, 0.0)
            spread_re, spread_im = substep(halves, order, first, last)
            waves[order, :, 0:8, :] = waves[order, :, R : R + 8, :]
            halves[order, :, 0:8, :] = halves[order, :, R : R + 8, :]
            win_re = trans[strip, order, 0].astype(jnp.int32).astype(jnp.float32)
            win_im = trans[strip, order, 1].astype(jnp.int32).astype(jnp.float32)
            out_re = ((win_re * spread_re + win_im * spread_im) * (1.0 / FIX)).astype(jnp.bfloat16)
            out_im = ((win_re * spread_im - win_im * spread_re) * (1.0 / FIX)).astype(jnp.bfloat16)
            lag = 2 * (order + 1)
            tall[order, 0, R : 2 * R, :] = spread_re
            tall[order, 1, R : 2 * R, :] = spread_im
            spread_out[before, order] = tall[order, :, lag : lag + R, :].astype(jnp.bfloat16)
            tall[order, :, 0:R, :] = tall[order, :, R : 2 * R, :]

            @pl.when(jnp.logical_and(strip > 0, jnp.logical_and(group < LATE, member != G - 1 - order)))
            def _():
                send_spread(strip - 1, order)

            if order < G - 1:
                wave_re = out_re.astype(jnp.float32)
                wave_im = out_im.astype(jnp.float32)
            else:
                wave_out[before, 0] = out_re
                wave_out[before, 1] = out_im

        @pl.when(strip > 0)
        def _():
            spr_ref[member, strip - 1] = spread_out[strip - 1, mine]

        @pl.when(jnp.logical_and(strip > 0, group > 0))
        def _():
            pltpu.make_async_remote_copy(
                src_ref=wave_out.at[strip - 1],
                dst_ref=inbox.at[strip - 1],
                send_sem=wave_sent,
                recv_sem=in_sem.at[strip - 1],
                device_id=at(group - 1, member),
                device_id_type=MESH,
            ).start()

        return unused

    lax.fori_loop(0, S, one_strip, 0)

    @pl.when(group >= LATE)
    def _():
        def rest(strip, unused):
            for order in range(G):

                @pl.when(member != G - 1 - order)
                def _():
                    send_spread(strip, order)

            return unused

        lax.fori_loop(0, S - 1, rest, 0)

    pltpu.make_async_copy(windows.at[0 : G - 1], windows.at[0 : G - 1], trans_sent).wait()
    pltpu.make_async_copy(spr_ref.at[0 : G - 1], spr_ref.at[0 : G - 1], spr_sent).wait()

    @pl.when(group > 0)
    def _():
        pltpu.make_async_copy(wave_out, wave_out, wave_sent).wait()

    pltpu.make_async_copy(spr_ref.at[0 : G - 1], spr_ref.at[0 : G - 1], spr_sem).wait()


def sweep(windows, exit_wave):
    return pl.pallas_call(
        sweep_kernel,
        out_shape=jax.ShapeDtypeStruct((G, S - 1, 2, R, W), jnp.bfloat16),
        in_specs=[pl.BlockSpec(memory_space=pltpu.VMEM)] * 2,
        out_specs=pl.BlockSpec(memory_space=pltpu.VMEM),
        scratch_shapes=[
            pltpu.VMEM((S, G, 2, R, W), HELD),
            pltpu.VMEM((S, 2, R, W), jnp.bfloat16),
            pltpu.VMEM((S - 1, G, 2, R, W), jnp.bfloat16),
            pltpu.VMEM((S - 1, 2, R, W), jnp.bfloat16),
            pltpu.VMEM((G, 2, R + 8, W), jnp.float32),
            pltpu.VMEM((G, 2, R + 8, W), jnp.float32),
            pltpu.VMEM((G, 2, 2 * R, W), jnp.float32),
            pltpu.SemaphoreType.DMA((S,)),
            pltpu.SemaphoreType.DMA((S - 1,)),
            pltpu.SemaphoreType.DMA,
            pltpu.SemaphoreType.DMA,
            pltpu.SemaphoreType.DMA,
            pltpu.SemaphoreType.DMA,
        ],
        compiler_params=pltpu.CompilerParams(collective_id=0, has_side_effects=True),
        name="sweep",
    )(windows, exit_wave)


def gather_kernel(offs_ref, fwd_ref, spr_ref, grad_ref, acc):
    acc[...] = jnp.zeros_like(acc)

    def per_position(position, unused):
        row_at = offs_ref[position, 0]
        col_at = offs_ref[position, 1]
        base = pl.multiple_of(col_at // 128 * 128, 128)

        def per_strip(strip, unused):
            rows = pl.ds(pl.multiple_of(strip * R, R), R)
            to = pl.ds(pl.multiple_of((row_at // 8 * 8) + strip * R, 8), R + 8)
            fwd_re = fwd_ref[position, 0, rows, :].astype(jnp.float32)
            fwd_im = fwd_ref[position, 1, rows, :].astype(jnp.float32)
            spread_re = spr_ref[position, strip, 0].astype(jnp.float32)
            spread_im = spr_ref[position, strip, 1].astype(jnp.float32)
            here = (fwd_re * spread_re + fwd_im * spread_im, fwd_re * spread_im - fwd_im * spread_re)
            for part in range(2):
                tiles = [
                    turned(
                        [here[part][8 * i : 8 * i + 8, 128 * j : 128 * j + 128] for j in range(2)],
                        lax.rem(col_at, 128),
                        1,
                        False,
                    )
                    for i in range(R // 8)
                ]
                columns = [
                    jnp.concatenate(turned([tile[j] for tile in tiles], lax.rem(row_at, 8), 0, False), axis=0)
                    for j in range(3)
                ]
                acc[part, to, pl.ds(base, 384)] += jnp.concatenate(columns, axis=1)
            return unused

        lax.fori_loop(0, S - 1, per_strip, 0)
        return unused

    lax.fori_loop(0, G, per_position, 0)
    grad_ref[...] = acc[:, 0:OBJ, 0:OBJ]


def gather(offsets, forward, spread):
    return pl.pallas_call(
        gather_kernel,
        out_shape=jax.ShapeDtypeStruct((2, OBJ, OBJ), jnp.float32),
        in_specs=[
            pl.BlockSpec(memory_space=pltpu.SMEM),
            pl.BlockSpec(memory_space=pltpu.VMEM),
            pl.BlockSpec(memory_space=pltpu.VMEM),
        ],
        out_specs=pl.BlockSpec(memory_space=pltpu.VMEM),
        scratch_shapes=[pltpu.VMEM((2, OBJ + 8, COLS), jnp.float32)],
        name="gather",
    )(offsets, forward, spread)


def reduce_kernel(grad_ref, out_ref, leaving, landing, sent, come):
    scan = lax.axis_index("scan")
    partner = (lax.axis_index("sec"), 1 - scan)
    barrier = pltpu.get_barrier_semaphore()
    pl.semaphore_signal(barrier, 1, device_id=partner, device_id_type=MESH)

    def chunk(block):
        return pltpu.make_async_remote_copy(
            src_ref=leaving.at[block],
            dst_ref=landing.at[block],
            send_sem=sent.at[block],
            recv_sem=come.at[block],
            device_id=partner,
            device_id_type=MESH,
        )

    pl.semaphore_wait(barrier, 1)

    def give(block, unused):
        rows = pl.ds(pl.multiple_of((1 - scan) * (OBJ // 2) + block * BLOCK, BLOCK), BLOCK)
        leaving[block] = grad_ref[:, rows, :].astype(jnp.bfloat16)
        chunk(block).start()
        return unused

    def join(block, unused):
        chunk(block).wait()
        rows = pl.ds(pl.multiple_of(scan * (OBJ // 2) + block * BLOCK, BLOCK), BLOCK)
        to = pl.ds(pl.multiple_of(block * BLOCK, BLOCK), BLOCK)
        out_ref[:, to, :] = grad_ref[:, rows, :] + landing[block].astype(jnp.float32)
        return unused

    lax.fori_loop(0, BLOCKS, give, 0)
    lax.fori_loop(0, BLOCKS, join, 0)


def reduce(gradient):
    return pl.pallas_call(
        reduce_kernel,
        out_shape=jax.ShapeDtypeStruct((2, OBJ // 2, OBJ), jnp.float32),
        in_specs=[pl.BlockSpec(memory_space=pltpu.VMEM)],
        out_specs=pl.BlockSpec(memory_space=pltpu.VMEM),
        scratch_shapes=[
            pltpu.VMEM((BLOCKS, 2, BLOCK, OBJ), jnp.bfloat16),
            pltpu.VMEM((BLOCKS, 2, BLOCK, OBJ), jnp.bfloat16),
            pltpu.SemaphoreType.DMA((BLOCKS,)),
            pltpu.SemaphoreType.DMA((BLOCKS,)),
        ],
        compiler_params=pltpu.CompilerParams(collective_id=2, has_side_effects=True),
        name="reduce",
    )(gradient)


def on_device(obj_amp, obj_phase, forward_waves, exit_adjoint, offsets):
    trans = jnp.concatenate([obj_amp * jnp.cos(obj_phase), obj_amp * jnp.sin(obj_phase)])
    half = jnp.round(trans * FIX).astype(jnp.int32).astype(HELD)
    member = lax.rem(lax.axis_index("sec"), G)
    own = lax.dynamic_index_in_dim(exit_adjoint, member, 0, keepdims=False)
    own = jnp.transpose(own.reshape(2, W // R, R, W), (1, 0, 2, 3))
    spread = sweep(extract(offsets, half, swap(half)), own)
    return reduce(gather(offsets, forward_waves[0], spread))[None]


def solution(mesh):
    in_specs = (
        P("sec", "scan", None),
        P("sec", "scan", None),
        P("sec", "scan", None, None, None),
        P("scan", None, None, None),
        P("scan", None),
    )
    out_specs = P("sec", None, "scan", None)
    return jax.shard_map(
        on_device, mesh=mesh, in_specs=in_specs, out_specs=out_specs, check_vma=False
    )
```

```python
import functools

import jax
import jax.numpy as jnp
from jax import lax
from jax.experimental import pallas as pl
from jax.experimental.pallas import tpu as pltpu
from jax.sharding import PartitionSpec as P

MESH = pl.DeviceIdType.MESH

damping = 0.0005
turning = 0.011

G = 8
R = 16
SKEW = 2 * G
W = 256
OBJ = 512
S = (W + SKEW) // R
TOP = 16
ROWS = OBJ + 40
LATE = 5
COLS = OBJ + 128
FIX = 32767.0
HELD = jnp.int16
BLOCK = 32
BLOCKS = OBJ // 2 // BLOCK


def swap_kernel(amp_ref, phase_ref, half_ref, other_ref, sent, come):
    partner = (lax.axis_index("sec"), 1 - lax.axis_index("scan"))
    barrier = pltpu.get_barrier_semaphore()
    pl.semaphore_signal(barrier, 1, device_id=partner, device_id_type=MESH)
    pl.semaphore_wait(barrier, 1)

    def chunk(block):
        rows = pl.ds(pl.multiple_of(block * BLOCK, BLOCK), BLOCK)
        return pltpu.make_async_remote_copy(
            src_ref=half_ref.at[:, rows, :],
            dst_ref=other_ref.at[:, rows, :],
            send_sem=sent.at[block],
            recv_sem=come.at[block],
            device_id=partner,
            device_id_type=MESH,
        )

    def fixed(value):
        value = value * FIX
        return jnp.where(value >= 0.0, value + 0.5, value - 0.5).astype(jnp.int32).astype(HELD)

    def give(block, unused):
        rows = pl.ds(pl.multiple_of(block * BLOCK, BLOCK), BLOCK)
        amp = amp_ref[rows, :]
        phase = phase_ref[rows, :]
        half_ref[0, rows, :] = fixed(amp * jnp.cos(phase))
        half_ref[1, rows, :] = fixed(amp * jnp.sin(phase))
        chunk(block).start()
        return unused

    def take(block, unused):
        chunk(block).wait()
        return unused

    lax.fori_loop(0, BLOCKS, give, 0)
    lax.fori_loop(0, BLOCKS, take, 0)


def swap(amp, phase):
    rows = jax.ShapeDtypeStruct((2, OBJ // 2, OBJ), HELD)
    return pl.pallas_call(
        swap_kernel,
        out_shape=(rows, rows),
        in_specs=[pl.BlockSpec(memory_space=pltpu.VMEM)] * 2,
        out_specs=[pl.BlockSpec(memory_space=pltpu.VMEM)] * 2,
        scratch_shapes=[pltpu.SemaphoreType.DMA((BLOCKS,)), pltpu.SemaphoreType.DMA((BLOCKS,))],
        compiler_params=pltpu.CompilerParams(collective_id=1, has_side_effects=True),
        name="swap",
    )(amp, phase)


def extract_kernel(offs_ref, half_ref, other_ref, win_ref, padded):
    scan = lax.axis_index("scan")
    order = G - 1 - lax.rem(lax.axis_index("sec"), G)
    delay = 2 * (order + 1)

    def place(source, start):
        def some_rows(block, unused):
            rows = pl.ds(pl.multiple_of(block * BLOCK, BLOCK), BLOCK)
            to = pl.ds(pl.multiple_of(start + block * BLOCK, 8), BLOCK)
            for part in range(2):
                for j in range(OBJ // 128):
                    padded[part, j, to, :] = source[part, rows, 128 * j : 128 * j + 128].astype(jnp.int32)
            return unused

        lax.fori_loop(0, BLOCKS, some_rows, 0)

    place(half_ref, pl.multiple_of(TOP + scan * (OBJ // 2), 8))
    place(other_ref, pl.multiple_of(TOP + (1 - scan) * (OBJ // 2), 8))
    lane = lax.broadcasted_iota(jnp.int32, (R, 128), 1)

    def per_strip(strip, unused):
        at = lax.broadcasted_iota(jnp.int32, (R, 128), 0) + (strip * R - delay)
        inside = jnp.logical_and(at >= 0, at < W)
        for position in range(G):
            col_at = offs_ref[position, 1]
            column = col_at // 128
            over = lax.rem(col_at, 128)
            turn = lax.rem(128 - over, 128)
            keep = lane < 128 - over
            rows = pl.ds(offs_ref[position, 0] + (strip * R - delay + TOP), R)
            for part in range(2):
                rolled = [pltpu.roll(padded[part, column + j, rows, :], turn, 1) for j in range(3)]
                for j in range(2):
                    value = jnp.where(inside, jnp.where(keep, rolled[j], rolled[j + 1]), 0)
                    win_ref[position, strip, part, :, 128 * j : 128 * j + 128] = value.astype(HELD)
        return unused

    lax.fori_loop(0, S, per_strip, 0)


def extract(offsets, half, other):
    return pl.pallas_call(
        extract_kernel,
        out_shape=jax.ShapeDtypeStruct((G, S, 2, R, W), HELD),
        in_specs=[
            pl.BlockSpec(memory_space=pltpu.SMEM),
            pl.BlockSpec(memory_space=pltpu.VMEM),
            pl.BlockSpec(memory_space=pltpu.VMEM),
        ],
        out_specs=pl.BlockSpec(memory_space=pltpu.VMEM),
        scratch_shapes=[pltpu.VMEM((2, OBJ // 128 + 1, ROWS, 128), jnp.int32)],
        name="extract",
    )(offsets, half, other)


def substep(buf, order, rows, new, first, last):
    mids, laps = [], []
    for part in range(2):
        mid = [buf[order, part, j, pl.ds(rows - 1, R), :] for j in range(2)]
        far = [buf[order, part, j, pl.ds(rows - 2, R), :] for j in range(2)]
        left = [pltpu.roll(mid[j], 1, 1) for j in range(2)]
        right = [pltpu.roll(mid[j], 127, 1) for j in range(2)]
        left = [jnp.where(first, 0.0, left[0]), jnp.where(first, left[0], left[1])]
        right = [jnp.where(last, right[1], right[0]), jnp.where(last, 0.0, right[1])]
        mids.append(mid)
        laps.append([(far[j] + new[part][j]) + (left[j] + right[j]) - 4.0 * mid[j] for j in range(2)])
    new_re = [mids[0][j] + damping * laps[0][j] + turning * laps[1][j] for j in range(2)]
    new_im = [mids[1][j] + damping * laps[1][j] - turning * laps[0][j] for j in range(2)]
    return new_re, new_im


def sweep_kernel(
    windows, exit_ref, spr_ref, trans, inbox, spread_out, wave_out, waves, halves, tall, mine_only,
    own_sem, exit_sem, trans_sem, in_sem, spr_sem, trans_sent, spr_sent, wave_sent,
):
    sec = lax.axis_index("sec")
    scan = lax.axis_index("scan")
    group = sec // G
    member = lax.rem(sec, G)
    groups = lax.axis_size("sec") // G
    top = group == groups - 1

    def at(g, m):
        return (g * G + m, scan)

    barrier = pltpu.get_barrier_semaphore()
    for step in range(1, G):
        pl.semaphore_signal(barrier, 1, device_id=at(group, lax.rem(member + step, G)), device_id_type=MESH)

    @pl.when(group > 0)
    def _():
        pl.semaphore_signal(barrier, 1, device_id=at(group - 1, member), device_id_type=MESH)

    @pl.when(jnp.logical_not(top))
    def _():
        pl.semaphore_signal(barrier, 1, device_id=at(group + 1, member), device_id_type=MESH)

    pl.semaphore_wait(barrier, G - 1 + jnp.where(group > 0, 1, 0) + jnp.where(top, 0, 1))
    for order in range(G):
        waves[order, :, :, 0:8, :] = jnp.zeros((2, 2, 8, 128), jnp.float32)
        halves[order, :, :, 0:8, :] = jnp.zeros((2, 2, 8, 128), jnp.float32)
    inbox[:, W:, :] = jnp.zeros((2, S * R - W, W), jnp.bfloat16)
    mine = G - 1 - member

    def give(strip, unused):
        for step in range(1, G):
            person = lax.rem(member + step, G)
            pltpu.make_async_remote_copy(
                src_ref=windows.at[person, strip],
                dst_ref=trans.at[strip, mine],
                send_sem=trans_sent,
                recv_sem=trans_sem.at[strip],
                device_id=at(group, person),
                device_id_type=MESH,
            ).start()
        return unused

    lax.fori_loop(0, S, give, 0)

    ours = pltpu.make_async_copy(windows.at[member], mine_only, own_sem)
    ours.start()

    @pl.when(top)
    def _():
        exits = pltpu.make_async_copy(exit_ref.at[member], inbox.at[:, 0:W, :], exit_sem)
        exits.start()
        exits.wait()

    ours.wait()

    def own(strip, unused):
        trans[strip, mine] = mine_only[strip]
        return unused

    lax.fori_loop(0, S, own, 0)
    lane = lax.broadcasted_iota(jnp.int32, (R, 128), 1)
    first = lane == 0
    last = lane == 127
    row = lax.broadcasted_iota(jnp.int32, (R, 128), 0)

    def send_spread(strip, order):
        pltpu.make_async_remote_copy(
            src_ref=spread_out.at[strip, order],
            dst_ref=spr_ref.at[member, strip],
            send_sem=spr_sent,
            recv_sem=spr_sem,
            device_id=at(group, G - 1 - order),
            device_id_type=MESH,
        ).start()

    def one_strip(strip, unused):
        @pl.when(jnp.logical_and(strip < S - 1, jnp.logical_not(top)))
        def _():
            landed = inbox.at[:, pl.ds(pl.multiple_of(strip * R, R), R), :]
            pltpu.make_async_copy(landed, landed, in_sem.at[strip]).wait()

        pltpu.make_async_copy(
            trans.at[strip, 0 : G - 1], trans.at[strip, 0 : G - 1], trans_sem.at[strip]
        ).wait()
        before = jnp.maximum(strip - 1, 0)
        at_strip = pl.multiple_of(strip * R, R)
        rows = pl.multiple_of(8 + strip * R, 8)
        seen = pl.multiple_of(before * R, R)
        wave = [
            [inbox[part, pl.ds(at_strip, R), 128 * j : 128 * j + 128].astype(jnp.float32) for j in range(2)]
            for part in range(2)
        ]
        for order in range(G):
            for part in range(2):
                for j in range(2):
                    waves[order, part, j, pl.ds(rows, R), :] = wave[part][j]
            half = substep(waves, order, rows, wave, first, last)
            at_row = row + (strip * R - 2 * order - 1)
            inside = jnp.logical_and(at_row >= 0, at_row < W)
            half = [[jnp.where(inside, half[part][j], 0.0) for j in range(2)] for part in range(2)]
            for part in range(2):
                for j in range(2):
                    halves[order, part, j, pl.ds(rows, R), :] = half[part][j]
            spread_re, spread_im = substep(halves, order, rows, half, first, last)
            lag = 2 * (order + 1)
            wave = [[], []]
            for j in range(2):
                cols = slice(128 * j, 128 * j + 128)
                tall[order, 0, j, pl.ds(at_strip, R), :] = spread_re[j]
                tall[order, 1, j, pl.ds(at_strip, R), :] = spread_im[j]
                win_re = trans[strip, order, 0, :, cols].astype(jnp.int32).astype(jnp.float32)
                win_im = trans[strip, order, 1, :, cols].astype(jnp.int32).astype(jnp.float32)
                out_re = ((win_re * spread_re[j] + win_im * spread_im[j]) * (1.0 / FIX)).astype(jnp.bfloat16)
                out_im = ((win_re * spread_im[j] - win_im * spread_re[j]) * (1.0 / FIX)).astype(jnp.bfloat16)
                if order < G - 1:
                    wave[0].append(out_re.astype(jnp.float32))
                    wave[1].append(out_im.astype(jnp.float32))
                else:
                    wave_out[before, 0, :, cols] = out_re
                    wave_out[before, 1, :, cols] = out_im

        @pl.when(jnp.logical_and(strip > 0, group > 0))
        def _():
            pltpu.make_async_remote_copy(
                src_ref=wave_out.at[strip - 1],
                dst_ref=inbox.at[:, pl.ds(seen, R), :],
                send_sem=wave_sent,
                recv_sem=in_sem.at[strip - 1],
                device_id=at(group - 1, member),
                device_id_type=MESH,
            ).start()

        for order in range(G):
            lag = 2 * (order + 1)
            for part in range(2):
                for j in range(2):
                    spread_out[before, order, part, :, 128 * j : 128 * j + 128] = tall[
                        order, part, j, pl.ds(seen + lag, R), :
                    ].astype(jnp.bfloat16)

            @pl.when(jnp.logical_and(strip > 0, jnp.logical_and(group < LATE, member != G - 1 - order)))
            def _():
                send_spread(strip - 1, order)

        @pl.when(strip > 0)
        def _():
            spr_ref[member, strip - 1] = spread_out[strip - 1, mine]

        return unused

    lax.fori_loop(0, S, one_strip, 0)

    @pl.when(group >= LATE)
    def _():
        def rest(strip, unused):
            for order in range(G):

                @pl.when(member != G - 1 - order)
                def _():
                    send_spread(strip, order)

            return unused

        lax.fori_loop(0, S - 1, rest, 0)

    pltpu.make_async_copy(windows.at[0 : G - 1], windows.at[0 : G - 1], trans_sent).wait()
    pltpu.make_async_copy(spr_ref.at[0 : G - 1], spr_ref.at[0 : G - 1], spr_sent).wait()

    @pl.when(group > 0)
    def _():
        pltpu.make_async_copy(wave_out, wave_out, wave_sent).wait()

    pltpu.make_async_copy(spr_ref.at[0 : G - 1], spr_ref.at[0 : G - 1], spr_sem).wait()


def sweep(windows, exit_adjoint):
    return pl.pallas_call(
        sweep_kernel,
        out_shape=jax.ShapeDtypeStruct((G, S - 1, 2, R, W), jnp.bfloat16),
        in_specs=[pl.BlockSpec(memory_space=pl.ANY)] * 2,
        out_specs=pl.BlockSpec(memory_space=pltpu.VMEM),
        scratch_shapes=[
            pltpu.VMEM((S, G, 2, R, W), HELD),
            pltpu.VMEM((2, S * R, W), jnp.bfloat16),
            pltpu.VMEM((S - 1, G, 2, R, W), jnp.bfloat16),
            pltpu.VMEM((S - 1, 2, R, W), jnp.bfloat16),
            pltpu.VMEM((G, 2, 2, 8 + S * R, 128), jnp.float32),
            pltpu.VMEM((G, 2, 2, 8 + S * R, 128), jnp.float32),
            pltpu.VMEM((G, 2, 2, S * R, 128), jnp.float32),
            pltpu.VMEM((S, 2, R, W), HELD),
            pltpu.SemaphoreType.DMA,
            pltpu.SemaphoreType.DMA,
            pltpu.SemaphoreType.DMA((S,)),
            pltpu.SemaphoreType.DMA((S - 1,)),
            pltpu.SemaphoreType.DMA,
            pltpu.SemaphoreType.DMA,
            pltpu.SemaphoreType.DMA,
            pltpu.SemaphoreType.DMA,
        ],
        compiler_params=pltpu.CompilerParams(collective_id=0, has_side_effects=True),
        name="sweep",
    )(windows, exit_adjoint)


def gather_kernel(offs_ref, fwd_ref, spr_ref, leave_ref, keep_ref, acc):
    scan = lax.axis_index("scan")
    acc[...] = jnp.zeros_like(acc)
    lane = lax.broadcasted_iota(jnp.int32, (R, 128), 1)

    def per_position(position, unused):
        row_at = offs_ref[position, 0]
        col_at = offs_ref[position, 1]
        column = col_at // 128
        over = lax.rem(col_at, 128)
        keep = lane >= over

        def per_strip(strip, unused):
            rows = pl.ds(pl.multiple_of(strip * R, R), R)
            to = pl.ds(row_at + strip * R, R)
            terms = [[], []]
            for j in range(2):
                cols = slice(128 * j, 128 * j + 128)
                fwd_re = fwd_ref[position, 0, rows, cols].astype(jnp.float32)
                fwd_im = fwd_ref[position, 1, rows, cols].astype(jnp.float32)
                spread_re = spr_ref[position, strip, 0, :, cols].astype(jnp.float32)
                spread_im = spr_ref[position, strip, 1, :, cols].astype(jnp.float32)
                terms[0].append(pltpu.roll(fwd_re * spread_re + fwd_im * spread_im, over, 1))
                terms[1].append(pltpu.roll(fwd_re * spread_im - fwd_im * spread_re, over, 1))
            for part in range(2):
                near, far = terms[part]
                acc[part, column, to, :] += jnp.where(keep, near, 0.0)
                acc[part, column + 1, to, :] += jnp.where(keep, far, near)
                acc[part, column + 2, to, :] += jnp.where(keep, 0.0, far)
            return unused

        lax.fori_loop(0, S - 1, per_strip, 0, unroll=2)
        return unused

    lax.fori_loop(0, G, per_position, 0)

    def split(block, unused):
        rows = pl.ds(pl.multiple_of(block * BLOCK, BLOCK), BLOCK)
        ours = pl.ds(pl.multiple_of(scan * (OBJ // 2) + block * BLOCK, BLOCK), BLOCK)
        theirs = pl.ds(pl.multiple_of((1 - scan) * (OBJ // 2) + block * BLOCK, BLOCK), BLOCK)
        for part in range(2):
            for j in range(OBJ // 128):
                leave_ref[block, part, :, 128 * j : 128 * j + 128] = acc[part, j, theirs, :].astype(jnp.bfloat16)
                keep_ref[part, rows, 128 * j : 128 * j + 128] = acc[part, j, ours, :]
        return unused

    lax.fori_loop(0, BLOCKS, split, 0)


def gather(offsets, forward, spread):
    return pl.pallas_call(
        gather_kernel,
        out_shape=(
            jax.ShapeDtypeStruct((BLOCKS, 2, BLOCK, OBJ), jnp.bfloat16),
            jax.ShapeDtypeStruct((2, OBJ // 2, OBJ), jnp.float32),
        ),
        in_specs=[
            pl.BlockSpec(memory_space=pltpu.SMEM),
            pl.BlockSpec(memory_space=pltpu.VMEM),
            pl.BlockSpec(memory_space=pltpu.VMEM),
        ],
        out_specs=[pl.BlockSpec(memory_space=pltpu.VMEM)] * 2,
        scratch_shapes=[pltpu.VMEM((2, OBJ // 128 + 1, OBJ, 128), jnp.float32)],
        name="gather",
    )(offsets, forward, spread)


def reduce_kernel(leave_ref, keep_ref, out_ref, landing, sent, come):
    scan = lax.axis_index("scan")
    partner = (lax.axis_index("sec"), 1 - scan)
    barrier = pltpu.get_barrier_semaphore()
    pl.semaphore_signal(barrier, 1, device_id=partner, device_id_type=MESH)
    pl.semaphore_wait(barrier, 1)

    def chunk(block):
        return pltpu.make_async_remote_copy(
            src_ref=leave_ref.at[block],
            dst_ref=landing.at[block],
            send_sem=sent.at[block],
            recv_sem=come.at[block],
            device_id=partner,
            device_id_type=MESH,
        )

    def give(block, unused):
        chunk(block).start()
        return unused

    def join(block, unused):
        chunk(block).wait()
        rows = pl.ds(pl.multiple_of(block * BLOCK, BLOCK), BLOCK)
        out_ref[:, rows, :] = keep_ref[:, rows, :] + landing[block].astype(jnp.float32)
        return unused

    lax.fori_loop(0, BLOCKS, give, 0)
    lax.fori_loop(0, BLOCKS, join, 0)


def reduce(leave, keep):
    return pl.pallas_call(
        reduce_kernel,
        out_shape=jax.ShapeDtypeStruct((2, OBJ // 2, OBJ), jnp.float32),
        in_specs=[pl.BlockSpec(memory_space=pltpu.VMEM)] * 2,
        out_specs=pl.BlockSpec(memory_space=pltpu.VMEM),
        scratch_shapes=[
            pltpu.VMEM((BLOCKS, 2, BLOCK, OBJ), jnp.bfloat16),
            pltpu.SemaphoreType.DMA((BLOCKS,)),
            pltpu.SemaphoreType.DMA((BLOCKS,)),
        ],
        compiler_params=pltpu.CompilerParams(collective_id=2, has_side_effects=True),
        name="reduce",
    )(leave, keep)


def on_device(obj_amp, obj_phase, forward_waves, exit_adjoint, offsets):
    half, other = swap(obj_amp[0], obj_phase[0])
    spread = sweep(extract(offsets, half, other), exit_adjoint)
    leave, keep = gather(offsets, forward_waves[0], spread)
    return reduce(leave, keep)[None]


def solution(mesh):
    in_specs = (
        P("sec", "scan", None),
        P("sec", "scan", None),
        P("sec", "scan", None, None, None),
        P("scan", None, None, None),
        P("scan", None),
    )
    out_specs = P("sec", None, "scan", None)
    return jax.shard_map(
        on_device, mesh=mesh, in_specs=in_specs, out_specs=out_specs, check_vma=False
    )
```

```python
import functools

import jax
import jax.numpy as jnp
from jax import lax
from jax.experimental import pallas as pl
from jax.experimental.pallas import tpu as pltpu
from jax.sharding import PartitionSpec as P

MESH = pl.DeviceIdType.MESH

damping = 0.0005
turning = 0.011

G = 8
R = 16
SKEW = 2 * G
W = 256
OBJ = 512
S = (W + SKEW) // R
TOP = 16
ROWS = OBJ + 40
LATE = 5
COLS = OBJ + 128
FIX = 32767.0
HELD = jnp.int16
RUN = 64
BLOCK = 32
BLOCKS = OBJ // 2 // BLOCK


def swap_kernel(amp_ref, phase_ref, half_ref, other_ref, sent, come):
    partner = (lax.axis_index("sec"), 1 - lax.axis_index("scan"))
    barrier = pltpu.get_barrier_semaphore()
    pl.semaphore_signal(barrier, 1, device_id=partner, device_id_type=MESH)
    pl.semaphore_wait(barrier, 1)

    def chunk(block):
        rows = pl.ds(pl.multiple_of(block * BLOCK, BLOCK), BLOCK)
        return pltpu.make_async_remote_copy(
            src_ref=half_ref.at[:, rows, :],
            dst_ref=other_ref.at[:, rows, :],
            send_sem=sent.at[block],
            recv_sem=come.at[block],
            device_id=partner,
            device_id_type=MESH,
        )

    def fixed(value):
        value = value * FIX
        return jnp.where(value >= 0.0, value + 0.5, value - 0.5).astype(jnp.int32).astype(HELD)

    def give(block, unused):
        rows = pl.ds(pl.multiple_of(block * BLOCK, BLOCK), BLOCK)
        amp = amp_ref[rows, :]
        phase = phase_ref[rows, :]
        half_ref[0, rows, :] = fixed(amp * jnp.cos(phase))
        half_ref[1, rows, :] = fixed(amp * jnp.sin(phase))
        chunk(block).start()
        return unused

    def take(block, unused):
        chunk(block).wait()
        return unused

    lax.fori_loop(0, BLOCKS, give, 0)
    lax.fori_loop(0, BLOCKS, take, 0)


def swap(amp, phase):
    rows = jax.ShapeDtypeStruct((2, OBJ // 2, OBJ), HELD)
    return pl.pallas_call(
        swap_kernel,
        out_shape=(rows, rows),
        in_specs=[pl.BlockSpec(memory_space=pltpu.VMEM)] * 2,
        out_specs=[pl.BlockSpec(memory_space=pltpu.VMEM)] * 2,
        scratch_shapes=[pltpu.SemaphoreType.DMA((BLOCKS,)), pltpu.SemaphoreType.DMA((BLOCKS,))],
        compiler_params=pltpu.CompilerParams(collective_id=1, has_side_effects=True),
        name="swap",
    )(amp, phase)


def extract_kernel(offs_ref, half_ref, other_ref, win_ref, padded):
    scan = lax.axis_index("scan")
    order = G - 1 - lax.rem(lax.axis_index("sec"), G)
    delay = 2 * (order + 1)

    def place(source, start):
        def some_rows(block, unused):
            rows = pl.ds(pl.multiple_of(block * BLOCK, BLOCK), BLOCK)
            to = pl.ds(pl.multiple_of(start + block * BLOCK, 8), BLOCK)
            for part in range(2):
                for j in range(OBJ // 128):
                    padded[part, j, to, :] = source[part, rows, 128 * j : 128 * j + 128].astype(jnp.int32)
            return unused

        lax.fori_loop(0, BLOCKS, some_rows, 0)

    place(half_ref, pl.multiple_of(TOP + scan * (OBJ // 2), 8))
    place(other_ref, pl.multiple_of(TOP + (1 - scan) * (OBJ // 2), 8))
    lane = lax.broadcasted_iota(jnp.int32, (R, 128), 1)

    def per_strip(strip, unused):
        at = lax.broadcasted_iota(jnp.int32, (R, 128), 0) + (strip * R - delay)
        inside = jnp.logical_and(at >= 0, at < W)
        for position in range(G):
            col_at = offs_ref[position, 1]
            column = col_at // 128
            over = lax.rem(col_at, 128)
            turn = lax.rem(128 - over, 128)
            keep = lane < 128 - over
            rows = pl.ds(offs_ref[position, 0] + (strip * R - delay + TOP), R)
            for part in range(2):
                rolled = [pltpu.roll(padded[part, column + j, rows, :], turn, 1) for j in range(3)]
                for j in range(2):
                    value = jnp.where(inside, jnp.where(keep, rolled[j], rolled[j + 1]), 0)
                    win_ref[position, strip, part, :, 128 * j : 128 * j + 128] = value.astype(HELD)
        return unused

    lax.fori_loop(0, S, per_strip, 0)


def extract(offsets, half, other):
    return pl.pallas_call(
        extract_kernel,
        out_shape=jax.ShapeDtypeStruct((G, S, 2, R, W), HELD),
        in_specs=[
            pl.BlockSpec(memory_space=pltpu.SMEM),
            pl.BlockSpec(memory_space=pltpu.VMEM),
            pl.BlockSpec(memory_space=pltpu.VMEM),
        ],
        out_specs=pl.BlockSpec(memory_space=pltpu.VMEM),
        scratch_shapes=[pltpu.VMEM((2, OBJ // 128 + 1, ROWS, 128), jnp.int32)],
        name="extract",
    )(offsets, half, other)


def behind(carry, at, value):
    top = lax.broadcasted_iota(jnp.int32, (8, 128), 0) < 1
    pieces = [carry[at]] + [value[8 * i : 8 * i + 8] for i in range(R // 8)]
    carry[at] = pieces[-1]
    rolled = [pltpu.roll(piece, 1, 0) for piece in pieces]
    return jnp.concatenate([jnp.where(top, rolled[i], rolled[i + 1]) for i in range(R // 8)], axis=0)


def times(re, im, value, j):
    return re * value[0][j] + im * value[1][j], re * value[1][j] - im * value[0][j]


def both_steps(carry, order, wave, inside, lane):
    sums, squares, here = [[], []], [[], []], [[], []]
    for part in range(2):
        v = wave[part]
        left1, left2 = ([pltpu.roll(v[j], n, 1) for j in range(2)] for n in (1, 2))
        right1, right2 = ([pltpu.roll(v[j], 128 - n, 1) for j in range(2)] for n in (1, 2))

        def pair(left, right, n):
            low, high = lane < n, lane >= 128 - n
            return [
                jnp.where(low, 0.0, left[0]) + jnp.where(high, right[1], right[0]),
                jnp.where(low, left[0], left[1]) + jnp.where(high, 0.0, right[1]),
            ]

        h = pair(left1, right1, 1)
        g = pair(left2, right2, 2)
        own = [jnp.where(lane == 0, 1.0, 2.0), jnp.where(lane == 127, 1.0, 2.0)]
        for j in range(2):
            g[j] = g[j] + own[j] * v[j]
            two = behind(carry, (order, 0, part, j), v[j])
            one = behind(carry, (order, 1, part, j), (h[j] - 4.0 * v[j]) + two)
            here[part].append(jnp.where(inside, v[j] + one, 0.0))
        sums[part] = h
        squares[part] = g
    square_re, square_im = damping * damping - turning * turning, 2.0 * damping * turning
    first_re, first_im = 2.0 * damping - 4.0 * square_re, 2.0 * turning - 4.0 * square_im
    inner = [[here[part][j] + squares[part][j] - 4.0 * sums[part][j] for j in range(2)] for part in range(2)]
    spread = [[], []]
    for j in range(2):
        last = times(square_re, square_im, here, j)
        middle = times(first_re, first_im, here, j)
        edge = times(square_re, square_im, sums, j)
        core = times(square_re, square_im, inner, j)
        for part in range(2):
            third = behind(carry, (order, 2, part, j), edge[part])
            second = behind(carry, (order, 3, part, j), (wave[part][j] + core[part]) + third)
            whole = behind(carry, (order, 4, part, j), (middle[part] + edge[part]) + second)
            spread[part].append(last[part] + whole)
    return spread


def sweep_kernel(
    windows, exit_ref, spr_ref, trans, inbox, spread_out, wave_out, waves, tall, mine_only,
    own_sem, exit_sem, trans_sem, in_sem, spr_sem, trans_sent, spr_sent, wave_sent,
):
    sec = lax.axis_index("sec")
    scan = lax.axis_index("scan")
    group = sec // G
    member = lax.rem(sec, G)
    groups = lax.axis_size("sec") // G
    top = group == groups - 1

    def at(g, m):
        return (g * G + m, scan)

    barrier = pltpu.get_barrier_semaphore()
    for step in range(1, G):
        pl.semaphore_signal(barrier, 1, device_id=at(group, lax.rem(member + step, G)), device_id_type=MESH)

    @pl.when(group > 0)
    def _():
        pl.semaphore_signal(barrier, 1, device_id=at(group - 1, member), device_id_type=MESH)

    @pl.when(jnp.logical_not(top))
    def _():
        pl.semaphore_signal(barrier, 1, device_id=at(group + 1, member), device_id_type=MESH)

    pl.semaphore_wait(barrier, G - 1 + jnp.where(group > 0, 1, 0) + jnp.where(top, 0, 1))
    waves[...] = jnp.zeros_like(waves)
    inbox[:, W:, :] = jnp.zeros((2, S * R - W, W), jnp.bfloat16)
    mine = G - 1 - member

    def give(strip, unused):
        for step in range(1, G):
            person = lax.rem(member + step, G)
            pltpu.make_async_remote_copy(
                src_ref=windows.at[person, strip],
                dst_ref=trans.at[strip, mine],
                send_sem=trans_sent,
                recv_sem=trans_sem.at[strip],
                device_id=at(group, person),
                device_id_type=MESH,
            ).start()
        return unused

    lax.fori_loop(0, S, give, 0)

    ours = pltpu.make_async_copy(windows.at[member], mine_only, own_sem)
    ours.start()

    @pl.when(top)
    def _():
        exits = pltpu.make_async_copy(exit_ref.at[member], inbox.at[:, 0:W, :], exit_sem)
        exits.start()
        exits.wait()

    ours.wait()

    def own(strip, unused):
        trans[strip, mine] = mine_only[strip]
        return unused

    lax.fori_loop(0, S, own, 0)
    lane = lax.broadcasted_iota(jnp.int32, (R, 128), 1)
    row = lax.broadcasted_iota(jnp.int32, (R, 128), 0)

    def send_spread(strip, order):
        pltpu.make_async_remote_copy(
            src_ref=spread_out.at[strip, order],
            dst_ref=spr_ref.at[member, strip],
            send_sem=spr_sent,
            recv_sem=spr_sem,
            device_id=at(group, G - 1 - order),
            device_id_type=MESH,
        ).start()

    def one_strip(strip, unused):
        @pl.when(jnp.logical_and(strip < S - 1, jnp.logical_not(top)))
        def _():
            landed = inbox.at[:, pl.ds(pl.multiple_of(strip * R, R), R), :]
            pltpu.make_async_copy(landed, landed, in_sem.at[strip]).wait()

        pltpu.make_async_copy(
            trans.at[strip, 0 : G - 1], trans.at[strip, 0 : G - 1], trans_sem.at[strip]
        ).wait()
        before = jnp.maximum(strip - 1, 0)
        at_strip = pl.multiple_of(strip * R, R)
        seen = pl.multiple_of(before * R, R)
        wave = [
            [inbox[part, pl.ds(at_strip, R), 128 * j : 128 * j + 128].astype(jnp.float32) for j in range(2)]
            for part in range(2)
        ]
        for order in range(G):
            at_row = row + (strip * R - 2 * order - 1)
            inside = jnp.logical_and(at_row >= 0, at_row < W)
            spread_re, spread_im = both_steps(waves, order, wave, inside, lane)
            wave = [[], []]
            for j in range(2):
                cols = slice(128 * j, 128 * j + 128)
                tall[order, 0, j, pl.ds(at_strip, R), :] = spread_re[j]
                tall[order, 1, j, pl.ds(at_strip, R), :] = spread_im[j]
                win_re = trans[strip, order, 0, :, cols].astype(jnp.int32).astype(jnp.float32)
                win_im = trans[strip, order, 1, :, cols].astype(jnp.int32).astype(jnp.float32)
                out_re = ((win_re * spread_re[j] + win_im * spread_im[j]) * (1.0 / FIX)).astype(jnp.bfloat16)
                out_im = ((win_re * spread_im[j] - win_im * spread_re[j]) * (1.0 / FIX)).astype(jnp.bfloat16)
                if order < G - 1:
                    wave[0].append(out_re.astype(jnp.float32))
                    wave[1].append(out_im.astype(jnp.float32))
                else:
                    wave_out[before, 0, :, cols] = out_re
                    wave_out[before, 1, :, cols] = out_im

        @pl.when(jnp.logical_and(strip > 0, group > 0))
        def _():
            pltpu.make_async_remote_copy(
                src_ref=wave_out.at[strip - 1],
                dst_ref=inbox.at[:, pl.ds(seen, R), :],
                send_sem=wave_sent,
                recv_sem=in_sem.at[strip - 1],
                device_id=at(group - 1, member),
                device_id_type=MESH,
            ).start()

        for order in range(G):
            lag = 2 * (order + 1)
            for part in range(2):
                for j in range(2):
                    spread_out[before, order, part, :, 128 * j : 128 * j + 128] = tall[
                        order, part, j, pl.ds(seen + lag, R), :
                    ].astype(jnp.bfloat16)

            @pl.when(jnp.logical_and(strip > 0, jnp.logical_and(group < LATE, member != G - 1 - order)))
            def _():
                send_spread(strip - 1, order)

        @pl.when(strip > 0)
        def _():
            spr_ref[member, strip - 1] = spread_out[strip - 1, mine]

        return unused

    lax.fori_loop(0, S, one_strip, 0)

    @pl.when(group >= LATE)
    def _():
        def rest(strip, unused):
            for order in range(G):

                @pl.when(member != G - 1 - order)
                def _():
                    send_spread(strip, order)

            return unused

        lax.fori_loop(0, S - 1, rest, 0)

    pltpu.make_async_copy(windows.at[0 : G - 1], windows.at[0 : G - 1], trans_sent).wait()
    pltpu.make_async_copy(spr_ref.at[0 : G - 1], spr_ref.at[0 : G - 1], spr_sent).wait()

    @pl.when(group > 0)
    def _():
        pltpu.make_async_copy(wave_out, wave_out, wave_sent).wait()

    pltpu.make_async_copy(spr_ref.at[0 : G - 1], spr_ref.at[0 : G - 1], spr_sem).wait()


def sweep(windows, exit_adjoint):
    return pl.pallas_call(
        sweep_kernel,
        out_shape=jax.ShapeDtypeStruct((G, S - 1, 2, R, W), jnp.bfloat16),
        in_specs=[pl.BlockSpec(memory_space=pl.ANY)] * 2,
        out_specs=pl.BlockSpec(memory_space=pltpu.VMEM),
        scratch_shapes=[
            pltpu.VMEM((S, G, 2, R, W), HELD),
            pltpu.VMEM((2, S * R, W), jnp.bfloat16),
            pltpu.VMEM((S - 1, G, 2, R, W), jnp.bfloat16),
            pltpu.VMEM((S - 1, 2, R, W), jnp.bfloat16),
            pltpu.VMEM((G, 5, 2, 2, 8, 128), jnp.float32),
            pltpu.VMEM((G, 2, 2, S * R, 128), jnp.float32),
            pltpu.VMEM((S, 2, R, W), HELD),
            pltpu.SemaphoreType.DMA,
            pltpu.SemaphoreType.DMA,
            pltpu.SemaphoreType.DMA((S,)),
            pltpu.SemaphoreType.DMA((S - 1,)),
            pltpu.SemaphoreType.DMA,
            pltpu.SemaphoreType.DMA,
            pltpu.SemaphoreType.DMA,
            pltpu.SemaphoreType.DMA,
        ],
        compiler_params=pltpu.CompilerParams(collective_id=0, has_side_effects=True),
        name="sweep",
    )(windows, exit_adjoint)


def gather_kernel(other, offs_ref, fwd_ref, spr_ref, grad_ref, acc):
    scan = lax.axis_index("scan")
    start = ((1 - scan) if other else scan) * (OBJ // 2)
    acc[...] = jnp.zeros_like(acc)
    lane = lax.broadcasted_iota(jnp.int32, (RUN, 128), 1)

    def per_position(position, unused):
        row_at = offs_ref[position, 0]
        col_at = offs_ref[position, 1]
        column = col_at // 128
        over = lax.rem(col_at, 128)
        keep = lane >= over
        begin = jnp.maximum(start - row_at, 0) // RUN
        end = jnp.minimum((start + OBJ // 2 - row_at + RUN - 1) // RUN, W // RUN)

        def per_run(run, unused):
            rows = pl.ds(pl.multiple_of(run * RUN, RUN), RUN)
            to = pl.ds(row_at + run * RUN - start + RUN, RUN)
            terms = [[], []]
            for j in range(2):
                cols = slice(128 * j, 128 * j + 128)
                fwd_re = fwd_ref[position, 0, rows, cols].astype(jnp.float32)
                fwd_im = fwd_ref[position, 1, rows, cols].astype(jnp.float32)
                spread = [
                    jnp.concatenate([spr_ref[position, run * (RUN // R) + i, part, :, cols] for i in range(RUN // R)], axis=0)
                    for part in range(2)
                ]
                spread_re, spread_im = (part.astype(jnp.float32) for part in spread)
                terms[0].append(pltpu.roll(fwd_re * spread_re + fwd_im * spread_im, over, 1))
                terms[1].append(pltpu.roll(fwd_re * spread_im - fwd_im * spread_re, over, 1))
            for part in range(2):
                near, far = terms[part]
                acc[part, column, to, :] += jnp.where(keep, near, 0.0)
                acc[part, column + 1, to, :] += jnp.where(keep, far, near)
                acc[part, column + 2, to, :] += jnp.where(keep, 0.0, far)
            return unused

        lax.fori_loop(begin, end, per_run, 0)
        return unused

    lax.fori_loop(0, G, per_position, 0)

    def split(block, unused):
        rows = pl.ds(pl.multiple_of(block * BLOCK, BLOCK), BLOCK)
        source = pl.ds(pl.multiple_of(RUN + block * BLOCK, BLOCK), BLOCK)
        for part in range(2):
            for j in range(OBJ // 128):
                grad_ref[part, rows, 128 * j : 128 * j + 128] = acc[part, j, source, :].astype(grad_ref.dtype)
        return unused

    lax.fori_loop(0, BLOCKS, split, 0)


def gather(offsets, forward, spread, other):
    return pl.pallas_call(
        functools.partial(gather_kernel, other),
        out_shape=jax.ShapeDtypeStruct((2, OBJ // 2, OBJ), jnp.bfloat16 if other else jnp.float32),
        in_specs=[
            pl.BlockSpec(memory_space=pltpu.SMEM),
            pl.BlockSpec(memory_space=pltpu.VMEM),
            pl.BlockSpec(memory_space=pltpu.VMEM),
        ],
        out_specs=pl.BlockSpec(memory_space=pltpu.VMEM),
        scratch_shapes=[pltpu.VMEM((2, OBJ // 128 + 1, OBJ // 2 + 2 * RUN, 128), jnp.float32)],
        cost_estimate=pl.CostEstimate(flops=20_000_000, bytes_accessed=6_000_000, transcendentals=0),
        name="gather_other" if other else "gather_own",
    )(offsets, forward, spread)


def on_device(obj_amp, obj_phase, forward_waves, exit_adjoint, offsets):
    half, other = swap(obj_amp[0], obj_phase[0])
    spread = sweep(extract(offsets, half, other), exit_adjoint)
    leave = gather(offsets, forward_waves[0], spread, True)
    come = lax.ppermute(leave, "scan", [(0, 1), (1, 0)])
    keep = gather(offsets, forward_waves[0], spread, False)
    return (keep + come.astype(jnp.float32))[None]


def solution(mesh):
    in_specs = (
        P("sec", "scan", None),
        P("sec", "scan", None),
        P("sec", "scan", None, None, None),
        P("scan", None, None, None),
        P("scan", None),
    )
    out_specs = P("sec", None, "scan", None)
    return jax.shard_map(
        on_device, mesh=mesh, in_specs=in_specs, out_specs=out_specs, check_vma=False
    )
```

```python
import functools

import jax
import jax.numpy as jnp
from jax import lax
from jax.experimental import pallas as pl
from jax.experimental.pallas import tpu as pltpu
from jax.sharding import PartitionSpec as P

MESH = pl.DeviceIdType.MESH

damping = 0.0005
turning = 0.011

G = 8
R = 16
SKEW = 2 * G
W = 256
OBJ = 512
S = (W + SKEW) // R
TOP = 16
ROWS = OBJ + 40
LATE = 5
COLS = OBJ + 128
FIX = 32767.0
HELD = jnp.int16
RUN = 64
BLOCK = 32
BLOCKS = OBJ // 2 // BLOCK


def behind(carry, at, value):
    top = lax.broadcasted_iota(jnp.int32, (8, 128), 0) < 1
    pieces = [carry[at]] + [value[8 * i : 8 * i + 8] for i in range(R // 8)]
    carry[at] = pieces[-1]
    rolled = [pltpu.roll(piece, 1, 0) for piece in pieces]
    return jnp.concatenate([jnp.where(top, rolled[i], rolled[i + 1]) for i in range(R // 8)], axis=0)


def times(re, im, value, j):
    return re * value[0][j] + im * value[1][j], re * value[1][j] - im * value[0][j]


def both_steps(carry, order, wave, inside, lane):
    sums, squares, here = [[], []], [[], []], [[], []]
    for part in range(2):
        v = wave[part]
        left1, left2 = ([pltpu.roll(v[j], n, 1) for j in range(2)] for n in (1, 2))
        right1, right2 = ([pltpu.roll(v[j], 128 - n, 1) for j in range(2)] for n in (1, 2))

        def pair(left, right, n):
            low, high = lane < n, lane >= 128 - n
            return [
                jnp.where(low, 0.0, left[0]) + jnp.where(high, right[1], right[0]),
                jnp.where(low, left[0], left[1]) + jnp.where(high, 0.0, right[1]),
            ]

        h = pair(left1, right1, 1)
        g = pair(left2, right2, 2)
        own = [jnp.where(lane == 0, 1.0, 2.0), jnp.where(lane == 127, 1.0, 2.0)]
        for j in range(2):
            g[j] = g[j] + own[j] * v[j]
            two = behind(carry, (order, 0, part, j), v[j])
            one = behind(carry, (order, 1, part, j), (h[j] - 4.0 * v[j]) + two)
            here[part].append(jnp.where(inside, v[j] + one, 0.0))
        sums[part] = h
        squares[part] = g
    square_re, square_im = damping * damping - turning * turning, 2.0 * damping * turning
    first_re, first_im = 2.0 * damping - 4.0 * square_re, 2.0 * turning - 4.0 * square_im
    inner = [[here[part][j] + squares[part][j] - 4.0 * sums[part][j] for j in range(2)] for part in range(2)]
    spread = [[], []]
    for j in range(2):
        last = times(square_re, square_im, here, j)
        middle = times(first_re, first_im, here, j)
        edge = times(square_re, square_im, sums, j)
        core = times(square_re, square_im, inner, j)
        for part in range(2):
            third = behind(carry, (order, 2, part, j), edge[part])
            second = behind(carry, (order, 3, part, j), (wave[part][j] + core[part]) + third)
            whole = behind(carry, (order, 4, part, j), (middle[part] + edge[part]) + second)
            spread[part].append(last[part] + whole)
    return spread


def sweep_kernel(
    plan_ref, amp_ref, phase_ref, exit_ref, spr_ref, half, other, padded, windows, trans, inbox, spread_out, wave_out, waves, tall,
    half_sem, half_sent, exit_sem, trans_sem, in_sem, spr_sem, trans_sent, spr_sent, wave_sent,
):
    sec = lax.axis_index("sec")
    scan = lax.axis_index("scan")
    group = sec // G
    member = lax.rem(sec, G)
    groups = lax.axis_size("sec") // G
    top = group == groups - 1

    def at(g, m):
        return (g * G + m, scan)

    barrier = pltpu.get_barrier_semaphore()
    for step in range(1, G):
        pl.semaphore_signal(barrier, 1, device_id=at(group, lax.rem(member + step, G)), device_id_type=MESH)

    partner = (sec, 1 - scan)
    pl.semaphore_signal(barrier, 1, device_id=partner, device_id_type=MESH)

    @pl.when(group > 0)
    def _():
        pl.semaphore_signal(barrier, 1, device_id=at(group - 1, member), device_id_type=MESH)

    @pl.when(jnp.logical_not(top))
    def _():
        pl.semaphore_signal(barrier, 1, device_id=at(group + 1, member), device_id_type=MESH)

    pl.semaphore_wait(barrier, G + jnp.where(group > 0, 1, 0) + jnp.where(top, 0, 1))
    mine = G - 1 - member
    delay = 2 * (mine + 1)
    exits = pltpu.make_async_copy(exit_ref.at[member], inbox.at[:, 0:W, :], exit_sem)

    @pl.when(top)
    def _():
        exits.start()

    def block_rows(block):
        return pl.ds(pl.multiple_of(block * BLOCK, BLOCK), BLOCK)

    def chunk(part, block):
        return pltpu.make_async_remote_copy(
            src_ref=half.at[part, block_rows(block), :],
            dst_ref=other.at[part, block_rows(block), :],
            send_sem=half_sent.at[part, block],
            recv_sem=half_sem.at[part, block],
            device_id=partner,
            device_id_type=MESH,
        )

    def place(part, block, value, owner):
        to = pl.ds(pl.multiple_of(TOP + owner * (OBJ // 2) + block * BLOCK, 8), BLOCK)
        for j in range(OBJ // 128):
            padded[part, j, to, :] = value[:, 128 * j : 128 * j + 128]

    for part, wave in enumerate((jnp.cos, jnp.sin)):

        def make(block, unused):
            value = amp_ref[block_rows(block), :] * wave(phase_ref[block_rows(block), :]) * FIX
            value = jnp.where(value >= 0.0, value + 0.5, value - 0.5).astype(jnp.int32)
            half[part, block_rows(block), :] = value.astype(HELD)
            chunk(part, block).start()
            place(part, block, value, scan)
            return unused

        lax.fori_loop(0, BLOCKS, make, 0)
    waves[...] = jnp.zeros_like(waves)
    inbox[:, W:, :] = jnp.zeros((2, S * R - W, W), jnp.bfloat16)
    lane = lax.broadcasted_iota(jnp.int32, (R, 128), 1)

    for part in range(2):

        def take(block, unused):
            chunk(part, block).wait()
            place(part, block, other[part, block_rows(block), :].astype(jnp.int32), 1 - scan)
            return unused

        lax.fori_loop(0, BLOCKS, take, 0)

        def give(strip, unused):
            at_row = lax.broadcasted_iota(jnp.int32, (R, 128), 0) + (strip * R - delay)
            inside = jnp.logical_and(at_row >= 0, at_row < W)
            for position in range(G):
                keep = lane < 128 - plan_ref[position, 2]
                rows = pl.ds(plan_ref[position, 0] + (strip * R - delay + TOP), R)
                rolled = [
                    pltpu.roll(padded[part, plan_ref[position, 1] + j, rows, :], plan_ref[position, 3], 1) for j in range(3)
                ]
                for j in range(2):
                    value = jnp.where(inside, jnp.where(keep, rolled[j], rolled[j + 1]), 0)
                    windows[part, position, strip, :, 128 * j : 128 * j + 128] = value.astype(HELD)
            trans[part, strip, mine] = windows[part, member, strip]
            for step in range(1, G):
                person = lax.rem(member + step, G)
                pltpu.make_async_remote_copy(
                    src_ref=windows.at[part, person, strip],
                    dst_ref=trans.at[part, strip, mine],
                    send_sem=trans_sent,
                    recv_sem=trans_sem.at[part, strip],
                    device_id=at(group, person),
                    device_id_type=MESH,
                ).start()
            return unused

        lax.fori_loop(0, S, give, 0)

    @pl.when(top)
    def _():
        exits.wait()

    row = lax.broadcasted_iota(jnp.int32, (R, 128), 0)

    def send_spread(strip, order):
        pltpu.make_async_remote_copy(
            src_ref=spread_out.at[strip, order],
            dst_ref=spr_ref.at[member, strip],
            send_sem=spr_sent,
            recv_sem=spr_sem,
            device_id=at(group, G - 1 - order),
            device_id_type=MESH,
        ).start()

    def one_strip(strip, unused):
        @pl.when(jnp.logical_and(strip < S - 1, jnp.logical_not(top)))
        def _():
            landed = inbox.at[:, pl.ds(pl.multiple_of(strip * R, R), R), :]
            pltpu.make_async_copy(landed, landed, in_sem.at[strip]).wait()

        for part in range(2):
            come = trans.at[part, strip, 0 : G - 1]
            pltpu.make_async_copy(come, come, trans_sem.at[part, strip]).wait()
        before = jnp.maximum(strip - 1, 0)
        at_strip = pl.multiple_of(strip * R, R)
        seen = pl.multiple_of(before * R, R)
        wave = [
            [inbox[part, pl.ds(at_strip, R), 128 * j : 128 * j + 128].astype(jnp.float32) for j in range(2)]
            for part in range(2)
        ]
        for order in range(G):
            at_row = row + (strip * R - 2 * order - 1)
            inside = jnp.logical_and(at_row >= 0, at_row < W)
            spread_re, spread_im = both_steps(waves, order, wave, inside, lane)
            wave = [[], []]
            for j in range(2):
                cols = slice(128 * j, 128 * j + 128)
                tall[order, 0, j, pl.ds(at_strip, R), :] = spread_re[j]
                tall[order, 1, j, pl.ds(at_strip, R), :] = spread_im[j]
                win_re = trans[0, strip, order, :, cols].astype(jnp.int32).astype(jnp.float32)
                win_im = trans[1, strip, order, :, cols].astype(jnp.int32).astype(jnp.float32)
                out_re = ((win_re * spread_re[j] + win_im * spread_im[j]) * (1.0 / FIX)).astype(jnp.bfloat16)
                out_im = ((win_re * spread_im[j] - win_im * spread_re[j]) * (1.0 / FIX)).astype(jnp.bfloat16)
                if order < G - 1:
                    wave[0].append(out_re.astype(jnp.float32))
                    wave[1].append(out_im.astype(jnp.float32))
                else:
                    wave_out[before, 0, :, cols] = out_re
                    wave_out[before, 1, :, cols] = out_im

        @pl.when(jnp.logical_and(strip > 0, group > 0))
        def _():
            pltpu.make_async_remote_copy(
                src_ref=wave_out.at[strip - 1],
                dst_ref=inbox.at[:, pl.ds(seen, R), :],
                send_sem=wave_sent,
                recv_sem=in_sem.at[strip - 1],
                device_id=at(group - 1, member),
                device_id_type=MESH,
            ).start()

        for order in range(G):
            lag = 2 * (order + 1)
            for part in range(2):
                for j in range(2):
                    spread_out[before, order, part, :, 128 * j : 128 * j + 128] = tall[
                        order, part, j, pl.ds(seen + lag, R), :
                    ].astype(jnp.bfloat16)

            @pl.when(jnp.logical_and(strip > 0, jnp.logical_and(group < LATE, member != G - 1 - order)))
            def _():
                send_spread(strip - 1, order)

        @pl.when(strip > 0)
        def _():
            spr_ref[member, strip - 1] = spread_out[strip - 1, mine]

        return unused

    lax.fori_loop(0, S, one_strip, 0)

    @pl.when(group >= LATE)
    def _():
        def rest(strip, unused):
            for order in range(G):

                @pl.when(member != G - 1 - order)
                def _():
                    send_spread(strip, order)

            return unused

        lax.fori_loop(0, S - 1, rest, 0)

    pltpu.make_async_copy(windows.at[:, 0 : G - 1], windows.at[:, 0 : G - 1], trans_sent).wait()
    pltpu.make_async_copy(spr_ref.at[0 : G - 1], spr_ref.at[0 : G - 1], spr_sent).wait()

    @pl.when(group > 0)
    def _():
        pltpu.make_async_copy(wave_out, wave_out, wave_sent).wait()

    pltpu.make_async_copy(spr_ref.at[0 : G - 1], spr_ref.at[0 : G - 1], spr_sem).wait()


def sweep(plan, amp, phase, exit_adjoint):
    return pl.pallas_call(
        sweep_kernel,
        out_shape=jax.ShapeDtypeStruct((G, S - 1, 2, R, W), jnp.bfloat16),
        in_specs=[
            pl.BlockSpec(memory_space=pltpu.SMEM),
            pl.BlockSpec(memory_space=pltpu.VMEM),
            pl.BlockSpec(memory_space=pltpu.VMEM),
            pl.BlockSpec(memory_space=pl.ANY),
        ],
        out_specs=pl.BlockSpec(memory_space=pltpu.VMEM),
        scratch_shapes=[
            pltpu.VMEM((2, OBJ // 2, OBJ), HELD),
            pltpu.VMEM((2, OBJ // 2, OBJ), HELD),
            pltpu.VMEM((2, OBJ // 128 + 1, ROWS, 128), jnp.int32),
            pltpu.VMEM((2, G, S, R, W), HELD),
            pltpu.VMEM((2, S, G, R, W), HELD),
            pltpu.VMEM((2, S * R, W), jnp.bfloat16),
            pltpu.VMEM((S - 1, G, 2, R, W), jnp.bfloat16),
            pltpu.VMEM((S - 1, 2, R, W), jnp.bfloat16),
            pltpu.VMEM((G, 5, 2, 2, 8, 128), jnp.float32),
            pltpu.VMEM((G, 2, 2, S * R, 128), jnp.float32),
            pltpu.SemaphoreType.DMA((2, BLOCKS)),
            pltpu.SemaphoreType.DMA((2, BLOCKS)),
            pltpu.SemaphoreType.DMA,
            pltpu.SemaphoreType.DMA((2, S)),
            pltpu.SemaphoreType.DMA((S - 1,)),
            pltpu.SemaphoreType.DMA,
            pltpu.SemaphoreType.DMA,
            pltpu.SemaphoreType.DMA,
            pltpu.SemaphoreType.DMA,
        ],
        compiler_params=pltpu.CompilerParams(collective_id=0, has_side_effects=True),
        name="sweep",
    )(plan, amp, phase, exit_adjoint)


def gather_kernel(other, offs_ref, fwd_ref, spr_ref, grad_ref, acc):
    scan = lax.axis_index("scan")
    start = ((1 - scan) if other else scan) * (OBJ // 2)
    acc[...] = jnp.zeros_like(acc)
    lane = lax.broadcasted_iota(jnp.int32, (RUN, 128), 1)

    def per_position(position, unused):
        row_at = offs_ref[position, 0]
        col_at = offs_ref[position, 1]
        column = col_at // 128
        over = lax.rem(col_at, 128)
        keep = lane >= over
        begin = jnp.maximum(start - row_at, 0) // RUN
        end = jnp.minimum((start + OBJ // 2 - row_at + RUN - 1) // RUN, W // RUN)

        def per_run(run, unused):
            rows = pl.ds(pl.multiple_of(run * RUN, RUN), RUN)
            to = pl.ds(row_at + run * RUN - start + RUN, RUN)
            terms = [[], []]
            for j in range(2):
                cols = slice(128 * j, 128 * j + 128)
                fwd_re = fwd_ref[position, 0, rows, cols].astype(jnp.float32)
                fwd_im = fwd_ref[position, 1, rows, cols].astype(jnp.float32)
                spread = [
                    jnp.concatenate([spr_ref[position, run * (RUN // R) + i, part, :, cols] for i in range(RUN // R)], axis=0)
                    for part in range(2)
                ]
                spread_re, spread_im = (part.astype(jnp.float32) for part in spread)
                terms[0].append(pltpu.roll(fwd_re * spread_re + fwd_im * spread_im, over, 1))
                terms[1].append(pltpu.roll(fwd_re * spread_im - fwd_im * spread_re, over, 1))
            for part in range(2):
                near, far = terms[part]
                acc[part, column, to, :] += jnp.where(keep, near, 0.0)
                acc[part, column + 1, to, :] += jnp.where(keep, far, near)
                acc[part, column + 2, to, :] += jnp.where(keep, 0.0, far)
            return unused

        lax.fori_loop(begin, end, per_run, 0)
        return unused

    lax.fori_loop(0, G, per_position, 0)

    def split(block, unused):
        rows = pl.ds(pl.multiple_of(block * BLOCK, BLOCK), BLOCK)
        source = pl.ds(pl.multiple_of(RUN + block * BLOCK, BLOCK), BLOCK)
        for part in range(2):
            for j in range(OBJ // 128):
                grad_ref[part, rows, 128 * j : 128 * j + 128] = acc[part, j, source, :].astype(grad_ref.dtype)
        return unused

    lax.fori_loop(0, BLOCKS, split, 0)


def gather(offsets, forward, spread, other):
    return pl.pallas_call(
        functools.partial(gather_kernel, other),
        out_shape=jax.ShapeDtypeStruct((2, OBJ // 2, OBJ), jnp.bfloat16 if other else jnp.float32),
        in_specs=[
            pl.BlockSpec(memory_space=pltpu.SMEM),
            pl.BlockSpec(memory_space=pltpu.VMEM),
            pl.BlockSpec(memory_space=pltpu.VMEM),
        ],
        out_specs=pl.BlockSpec(memory_space=pltpu.VMEM),
        scratch_shapes=[pltpu.VMEM((2, OBJ // 128 + 1, OBJ // 2 + 2 * RUN, 128), jnp.float32)],
        cost_estimate=pl.CostEstimate(flops=20_000_000, bytes_accessed=6_000_000, transcendentals=0),
        name="gather_other" if other else "gather_own",
    )(offsets, forward, spread)


def on_device(obj_amp, obj_phase, forward_waves, exit_adjoint, offsets):
    column, over = offsets[:, 1] // 128, offsets[:, 1] % 128
    plan = jnp.stack([offsets[:, 0], column, over, (128 - over) % 128], axis=1)
    spread = sweep(plan, obj_amp[0], obj_phase[0], exit_adjoint)
    leave = gather(offsets, forward_waves[0], spread, True)
    come = lax.ppermute(leave, "scan", [(0, 1), (1, 0)])
    keep = gather(offsets, forward_waves[0], spread, False)
    return (keep + come.astype(jnp.float32))[None]


def solution(mesh):
    in_specs = (
        P("sec", "scan", None),
        P("sec", "scan", None),
        P("sec", "scan", None, None, None),
        P("scan", None, None, None),
        P("scan", None),
    )
    out_specs = P("sec", None, "scan", None)
    return jax.shard_map(
        on_device, mesh=mesh, in_specs=in_specs, out_specs=out_specs, check_vma=False
    )
```

```python
import functools

import jax
import jax.numpy as jnp
from jax import lax
from jax.experimental import pallas as pl
from jax.experimental.pallas import tpu as pltpu
from jax.sharding import PartitionSpec as P

MESH = pl.DeviceIdType.MESH

damping = 0.0005
turning = 0.011

G = 8
R = 16
SKEW = 2 * G
W = 256
OBJ = 512
S = (W + SKEW) // R
TOP = 16
ROWS = OBJ + 40
AHEAD = 7
LATE = 5
COLS = OBJ + 128
FIX = 32767.0
HELD = jnp.int16
RUN = 64
BLOCK = 32
BLOCKS = OBJ // 2 // BLOCK


def behind(carry, at, value):
    top = lax.broadcasted_iota(jnp.int32, (8, 128), 0) < 1
    pieces = [carry[at]] + [value[8 * i : 8 * i + 8] for i in range(R // 8)]
    carry[at] = pieces[-1]
    rolled = [pltpu.roll(piece, 1, 0) for piece in pieces]
    return jnp.concatenate([jnp.where(top, rolled[i], rolled[i + 1]) for i in range(R // 8)], axis=0)


def times(re, im, value, j):
    return re * value[0][j] + im * value[1][j], re * value[1][j] - im * value[0][j]


def both_steps(carry, order, wave, inside, lane):
    sums, squares, here = [[], []], [[], []], [[], []]
    for part in range(2):
        v = wave[part]
        left1, left2 = ([pltpu.roll(v[j], n, 1) for j in range(2)] for n in (1, 2))
        right1, right2 = ([pltpu.roll(v[j], 128 - n, 1) for j in range(2)] for n in (1, 2))

        def pair(left, right, n):
            low, high = lane < n, lane >= 128 - n
            return [
                jnp.where(low, 0.0, left[0]) + jnp.where(high, right[1], right[0]),
                jnp.where(low, left[0], left[1]) + jnp.where(high, 0.0, right[1]),
            ]

        h = pair(left1, right1, 1)
        g = pair(left2, right2, 2)
        own = [jnp.where(lane == 0, 1.0, 2.0), jnp.where(lane == 127, 1.0, 2.0)]
        for j in range(2):
            g[j] = g[j] + own[j] * v[j]
            two = behind(carry, (order, 0, part, j), v[j])
            one = behind(carry, (order, 1, part, j), (h[j] - 4.0 * v[j]) + two)
            here[part].append(jnp.where(inside, v[j] + one, 0.0))
        sums[part] = h
        squares[part] = g
    square_re, square_im = damping * damping - turning * turning, 2.0 * damping * turning
    first_re, first_im = 2.0 * damping - 4.0 * square_re, 2.0 * turning - 4.0 * square_im
    inner = [[here[part][j] + squares[part][j] - 4.0 * sums[part][j] for j in range(2)] for part in range(2)]
    spread = [[], []]
    for j in range(2):
        last = times(square_re, square_im, here, j)
        middle = times(first_re, first_im, here, j)
        edge = times(square_re, square_im, sums, j)
        core = times(square_re, square_im, inner, j)
        for part in range(2):
            third = behind(carry, (order, 2, part, j), edge[part])
            second = behind(carry, (order, 3, part, j), (wave[part][j] + core[part]) + third)
            whole = behind(carry, (order, 4, part, j), (middle[part] + edge[part]) + second)
            spread[part].append(last[part] + whole)
    return spread


def sweep_kernel(
    plan_ref, amp_ref, phase_ref, exit_ref, spr_ref, half, other, padded, windows, trans, inbox, spread_out, wave_out, waves, tall,
    half_sem, half_sent, exit_sem, trans_sem, in_sem, spr_sem, trans_sent, spr_sent, wave_sent,
):
    sec = lax.axis_index("sec")
    scan = lax.axis_index("scan")
    group = sec // G
    member = lax.rem(sec, G)
    groups = lax.axis_size("sec") // G
    top = group == groups - 1

    def at(g, m):
        return (g * G + m, scan)

    barrier = pltpu.get_barrier_semaphore()
    for step in range(1, G):
        pl.semaphore_signal(barrier, 1, device_id=at(group, lax.rem(member + step, G)), device_id_type=MESH)

    partner = (sec, 1 - scan)
    pl.semaphore_signal(barrier, 1, device_id=partner, device_id_type=MESH)

    @pl.when(group > 0)
    def _():
        pl.semaphore_signal(barrier, 1, device_id=at(group - 1, member), device_id_type=MESH)

    @pl.when(jnp.logical_not(top))
    def _():
        pl.semaphore_signal(barrier, 1, device_id=at(group + 1, member), device_id_type=MESH)

    pl.semaphore_wait(barrier, G + jnp.where(group > 0, 1, 0) + jnp.where(top, 0, 1))
    mine = G - 1 - member
    delay = 2 * (mine + 1)
    exits = pltpu.make_async_copy(exit_ref.at[member], inbox.at[:, 0:W, :], exit_sem)

    @pl.when(top)
    def _():
        exits.start()

    def block_rows(block):
        return pl.ds(pl.multiple_of(block * BLOCK, BLOCK), BLOCK)

    def chunk(part, block):
        return pltpu.make_async_remote_copy(
            src_ref=half.at[part, block_rows(block), :],
            dst_ref=other.at[part, block_rows(block), :],
            send_sem=half_sent.at[part, block],
            recv_sem=half_sem.at[part, block],
            device_id=partner,
            device_id_type=MESH,
        )

    def place(part, block, value, owner):
        to = pl.ds(pl.multiple_of(TOP + owner * (OBJ // 2) + block * BLOCK, 8), BLOCK)
        for j in range(OBJ // 128):
            padded[part, j, to, :] = value[:, 128 * j : 128 * j + 128]

    for part, wave in enumerate((jnp.cos, jnp.sin)):

        def make(block, unused):
            value = amp_ref[block_rows(block), :] * wave(phase_ref[block_rows(block), :]) * FIX
            value = jnp.where(value >= 0.0, value + 0.5, value - 0.5).astype(jnp.int32)
            half[part, block_rows(block), :] = value.astype(HELD)
            chunk(part, block).start()
            place(part, block, value, scan)
            return unused

        lax.fori_loop(0, BLOCKS, make, 0)
    waves[...] = jnp.zeros_like(waves)
    inbox[:, W:, :] = jnp.zeros((2, S * R - W, W), jnp.bfloat16)
    lane = lax.broadcasted_iota(jnp.int32, (R, 128), 1)

    def take(part):
        def some_rows(block, unused):
            chunk(part, block).wait()
            place(part, block, other[part, block_rows(block), :].astype(jnp.int32), 1 - scan)
            return unused

        lax.fori_loop(0, BLOCKS, some_rows, 0)

    def give(strip, parts):
        at_row = lax.broadcasted_iota(jnp.int32, (R, 128), 0) + (strip * R - delay)
        inside = jnp.logical_and(at_row >= 0, at_row < W)
        for part in parts:
            for position in range(G):
                keep = lane < 128 - plan_ref[position, 2]
                rows = pl.ds(plan_ref[position, 0] + (strip * R - delay + TOP), R)
                rolled = [
                    pltpu.roll(padded[part, plan_ref[position, 1] + j, rows, :], plan_ref[position, 3], 1) for j in range(3)
                ]
                for j in range(2):
                    value = jnp.where(inside, jnp.where(keep, rolled[j], rolled[j + 1]), 0)
                    windows[part, position, strip, :, 128 * j : 128 * j + 128] = value.astype(HELD)
            trans[part, strip, mine] = windows[part, member, strip]
            for step in range(1, G):
                person = lax.rem(member + step, G)
                pltpu.make_async_remote_copy(
                    src_ref=windows.at[part, person, strip],
                    dst_ref=trans.at[part, strip, mine],
                    send_sem=trans_sent,
                    recv_sem=trans_sem.at[part, strip],
                    device_id=at(group, person),
                    device_id_type=MESH,
                ).start()

    def gives(begin, end, parts):
        def some_strips(strip, unused):
            give(strip, parts)
            return unused

        lax.fori_loop(begin, end, some_strips, 0)

    take(0)
    gives(0, AHEAD, (0,))
    take(1)
    gives(0, AHEAD, (1,))
    gives(AHEAD, S, (0, 1))

    @pl.when(top)
    def _():
        exits.wait()

    row = lax.broadcasted_iota(jnp.int32, (R, 128), 0)

    def send_spread(strip, order):
        pltpu.make_async_remote_copy(
            src_ref=spread_out.at[strip, order],
            dst_ref=spr_ref.at[member, strip],
            send_sem=spr_sent,
            recv_sem=spr_sem,
            device_id=at(group, G - 1 - order),
            device_id_type=MESH,
        ).start()

    def one_strip(strip, unused):
        @pl.when(jnp.logical_and(strip < S - 1, jnp.logical_not(top)))
        def _():
            landed = inbox.at[:, pl.ds(pl.multiple_of(strip * R, R), R), :]
            pltpu.make_async_copy(landed, landed, in_sem.at[strip]).wait()

        for part in range(2):
            come = trans.at[part, strip, 0 : G - 1]
            pltpu.make_async_copy(come, come, trans_sem.at[part, strip]).wait()
        before = jnp.maximum(strip - 1, 0)
        at_strip = pl.multiple_of(strip * R, R)
        seen = pl.multiple_of(before * R, R)
        wave = [
            [inbox[part, pl.ds(at_strip, R), 128 * j : 128 * j + 128].astype(jnp.float32) for j in range(2)]
            for part in range(2)
        ]
        for order in range(G):
            at_row = row + (strip * R - 2 * order - 1)
            inside = jnp.logical_and(at_row >= 0, at_row < W)
            spread_re, spread_im = both_steps(waves, order, wave, inside, lane)
            wave = [[], []]
            for j in range(2):
                cols = slice(128 * j, 128 * j + 128)
                tall[order, 0, j, pl.ds(at_strip, R), :] = spread_re[j]
                tall[order, 1, j, pl.ds(at_strip, R), :] = spread_im[j]
                win_re = trans[0, strip, order, :, cols].astype(jnp.int32).astype(jnp.float32)
                win_im = trans[1, strip, order, :, cols].astype(jnp.int32).astype(jnp.float32)
                out_re = ((win_re * spread_re[j] + win_im * spread_im[j]) * (1.0 / FIX)).astype(jnp.bfloat16)
                out_im = ((win_re * spread_im[j] - win_im * spread_re[j]) * (1.0 / FIX)).astype(jnp.bfloat16)
                if order < G - 1:
                    wave[0].append(out_re.astype(jnp.float32))
                    wave[1].append(out_im.astype(jnp.float32))
                else:
                    wave_out[before, 0, :, cols] = out_re
                    wave_out[before, 1, :, cols] = out_im

        @pl.when(jnp.logical_and(strip > 0, group > 0))
        def _():
            pltpu.make_async_remote_copy(
                src_ref=wave_out.at[strip - 1],
                dst_ref=inbox.at[:, pl.ds(seen, R), :],
                send_sem=wave_sent,
                recv_sem=in_sem.at[strip - 1],
                device_id=at(group - 1, member),
                device_id_type=MESH,
            ).start()

        for order in range(G):
            lag = 2 * (order + 1)
            for part in range(2):
                for j in range(2):
                    spread_out[before, order, part, :, 128 * j : 128 * j + 128] = tall[
                        order, part, j, pl.ds(seen + lag, R), :
                    ].astype(jnp.bfloat16)

            @pl.when(jnp.logical_and(strip > 0, jnp.logical_and(group < LATE, member != G - 1 - order)))
            def _():
                send_spread(strip - 1, order)

        @pl.when(strip > 0)
        def _():
            spr_ref[member, strip - 1] = spread_out[strip - 1, mine]

        return unused

    lax.fori_loop(0, S, one_strip, 0)

    @pl.when(group >= LATE)
    def _():
        def rest(strip, unused):
            for order in range(G):

                @pl.when(member != G - 1 - order)
                def _():
                    send_spread(strip, order)

            return unused

        lax.fori_loop(0, S - 1, rest, 0)

    pltpu.make_async_copy(windows.at[:, 0 : G - 1], windows.at[:, 0 : G - 1], trans_sent).wait()
    pltpu.make_async_copy(spr_ref.at[0 : G - 1], spr_ref.at[0 : G - 1], spr_sent).wait()

    @pl.when(group > 0)
    def _():
        pltpu.make_async_copy(wave_out, wave_out, wave_sent).wait()

    pltpu.make_async_copy(spr_ref.at[0 : G - 1], spr_ref.at[0 : G - 1], spr_sem).wait()


def sweep(plan, amp, phase, exit_adjoint):
    return pl.pallas_call(
        sweep_kernel,
        out_shape=jax.ShapeDtypeStruct((G, S - 1, 2, R, W), jnp.bfloat16),
        in_specs=[
            pl.BlockSpec(memory_space=pltpu.SMEM),
            pl.BlockSpec(memory_space=pltpu.VMEM),
            pl.BlockSpec(memory_space=pltpu.VMEM),
            pl.BlockSpec(memory_space=pl.ANY),
        ],
        out_specs=pl.BlockSpec(memory_space=pltpu.VMEM),
        scratch_shapes=[
            pltpu.VMEM((2, OBJ // 2, OBJ), HELD),
            pltpu.VMEM((2, OBJ // 2, OBJ), HELD),
            pltpu.VMEM((2, OBJ // 128 + 1, ROWS, 128), jnp.int32),
            pltpu.VMEM((2, G, S, R, W), HELD),
            pltpu.VMEM((2, S, G, R, W), HELD),
            pltpu.VMEM((2, S * R, W), jnp.bfloat16),
            pltpu.VMEM((S - 1, G, 2, R, W), jnp.bfloat16),
            pltpu.VMEM((S - 1, 2, R, W), jnp.bfloat16),
            pltpu.VMEM((G, 5, 2, 2, 8, 128), jnp.float32),
            pltpu.VMEM((G, 2, 2, S * R, 128), jnp.float32),
            pltpu.SemaphoreType.DMA((2, BLOCKS)),
            pltpu.SemaphoreType.DMA((2, BLOCKS)),
            pltpu.SemaphoreType.DMA,
            pltpu.SemaphoreType.DMA((2, S)),
            pltpu.SemaphoreType.DMA((S - 1,)),
            pltpu.SemaphoreType.DMA,
            pltpu.SemaphoreType.DMA,
            pltpu.SemaphoreType.DMA,
            pltpu.SemaphoreType.DMA,
        ],
        compiler_params=pltpu.CompilerParams(collective_id=0, has_side_effects=True),
        name="sweep",
    )(plan, amp, phase, exit_adjoint)


def gather_kernel(other, offs_ref, fwd_ref, spr_ref, grad_ref, acc):
    scan = lax.axis_index("scan")
    start = ((1 - scan) if other else scan) * (OBJ // 2)
    acc[...] = jnp.zeros_like(acc)
    lane = lax.broadcasted_iota(jnp.int32, (RUN, 128), 1)

    def per_position(position, unused):
        row_at = offs_ref[position, 0]
        col_at = offs_ref[position, 1]
        column = col_at // 128
        over = lax.rem(col_at, 128)
        keep = lane >= over
        begin = jnp.maximum(start - row_at, 0) // RUN
        end = jnp.minimum((start + OBJ // 2 - row_at + RUN - 1) // RUN, W // RUN)

        def per_run(run, unused):
            rows = pl.ds(pl.multiple_of(run * RUN, RUN), RUN)
            to = pl.ds(row_at + run * RUN - start + RUN, RUN)
            terms = [[], []]
            for j in range(2):
                cols = slice(128 * j, 128 * j + 128)
                fwd_re = fwd_ref[position, 0, rows, cols].astype(jnp.float32)
                fwd_im = fwd_ref[position, 1, rows, cols].astype(jnp.float32)
                spread = [
                    jnp.concatenate([spr_ref[position, run * (RUN // R) + i, part, :, cols] for i in range(RUN // R)], axis=0)
                    for part in range(2)
                ]
                spread_re, spread_im = (part.astype(jnp.float32) for part in spread)
                terms[0].append(pltpu.roll(fwd_re * spread_re + fwd_im * spread_im, over, 1))
                terms[1].append(pltpu.roll(fwd_re * spread_im - fwd_im * spread_re, over, 1))
            for part in range(2):
                near, far = terms[part]
                acc[part, column, to, :] += jnp.where(keep, near, 0.0)
                acc[part, column + 1, to, :] += jnp.where(keep, far, near)
                acc[part, column + 2, to, :] += jnp.where(keep, 0.0, far)
            return unused

        lax.fori_loop(begin, end, per_run, 0)
        return unused

    lax.fori_loop(0, G, per_position, 0)

    def split(block, unused):
        rows = pl.ds(pl.multiple_of(block * BLOCK, BLOCK), BLOCK)
        source = pl.ds(pl.multiple_of(RUN + block * BLOCK, BLOCK), BLOCK)
        for part in range(2):
            for j in range(OBJ // 128):
                grad_ref[part, rows, 128 * j : 128 * j + 128] = acc[part, j, source, :].astype(grad_ref.dtype)
        return unused

    lax.fori_loop(0, BLOCKS, split, 0)


def gather(offsets, forward, spread, other):
    return pl.pallas_call(
        functools.partial(gather_kernel, other),
        out_shape=jax.ShapeDtypeStruct((2, OBJ // 2, OBJ), jnp.bfloat16 if other else jnp.float32),
        in_specs=[
            pl.BlockSpec(memory_space=pltpu.SMEM),
            pl.BlockSpec(memory_space=pltpu.VMEM),
            pl.BlockSpec(memory_space=pltpu.VMEM),
        ],
        out_specs=pl.BlockSpec(memory_space=pltpu.VMEM),
        scratch_shapes=[pltpu.VMEM((2, OBJ // 128 + 1, OBJ // 2 + 2 * RUN, 128), jnp.float32)],
        cost_estimate=pl.CostEstimate(flops=20_000_000, bytes_accessed=6_000_000, transcendentals=0),
        name="gather_other" if other else "gather_own",
    )(offsets, forward, spread)


def on_device(obj_amp, obj_phase, forward_waves, exit_adjoint, offsets):
    column, over = offsets[:, 1] // 128, offsets[:, 1] % 128
    plan = jnp.stack([offsets[:, 0], column, over, (128 - over) % 128], axis=1)
    spread = sweep(plan, obj_amp[0], obj_phase[0], exit_adjoint)
    leave = gather(offsets, forward_waves[0], spread, True)
    come = lax.ppermute(leave, "scan", [(0, 1), (1, 0)])
    keep = gather(offsets, forward_waves[0], spread, False)
    return (keep + come.astype(jnp.float32))[None]


def solution(mesh):
    in_specs = (
        P("sec", "scan", None),
        P("sec", "scan", None),
        P("sec", "scan", None, None, None),
        P("scan", None, None, None),
        P("scan", None),
    )
    out_specs = P("sec", None, "scan", None)
    return jax.shard_map(
        on_device, mesh=mesh, in_specs=in_specs, out_specs=out_specs, check_vma=False
    )
```

```python
import functools

import jax
import jax.numpy as jnp
from jax import lax
from jax.experimental import pallas as pl
from jax.experimental.pallas import tpu as pltpu
from jax.sharding import PartitionSpec as P

MESH = pl.DeviceIdType.MESH

damping = 0.0005
turning = 0.011

G = 8
R = 16
SKEW = 2 * G
W = 256
OBJ = 512
S = (W + SKEW) // R
TOP = 16
ROWS = OBJ + 40
AHEAD = 7
LATE = 5
COLS = OBJ + 128
FIX = 32767.0
HELD = jnp.int16
RUN = 64
BLOCK = 32
BLOCKS = OBJ // 2 // BLOCK


def behind(carry, at, value):
    top = lax.broadcasted_iota(jnp.int32, (8, 128), 0) < 1
    pieces = [carry[at]] + [value[8 * i : 8 * i + 8] for i in range(R // 8)]
    carry[at] = pieces[-1]
    rolled = [pltpu.roll(piece, 1, 0) for piece in pieces]
    return jnp.concatenate([jnp.where(top, rolled[i], rolled[i + 1]) for i in range(R // 8)], axis=0)


def times(re, im, value, j):
    return re * value[0][j] + im * value[1][j], re * value[1][j] - im * value[0][j]


def both_steps(carry, order, wave, inside, lane):
    sums, squares, here = [[], []], [[], []], [[], []]
    for part in range(2):
        v = wave[part]
        left1, left2 = ([pltpu.roll(v[j], n, 1) for j in range(2)] for n in (1, 2))
        right1, right2 = ([pltpu.roll(v[j], 128 - n, 1) for j in range(2)] for n in (1, 2))

        def pair(left, right, n):
            low, high = lane < n, lane >= 128 - n
            return [
                jnp.where(low, 0.0, left[0]) + jnp.where(high, right[1], right[0]),
                jnp.where(low, left[0], left[1]) + jnp.where(high, 0.0, right[1]),
            ]

        h = pair(left1, right1, 1)
        g = pair(left2, right2, 2)
        own = [jnp.where(lane == 0, 1.0, 2.0), jnp.where(lane == 127, 1.0, 2.0)]
        for j in range(2):
            g[j] = g[j] + own[j] * v[j]
            two = behind(carry, (order, 0, part, j), v[j])
            one = behind(carry, (order, 1, part, j), (h[j] - 4.0 * v[j]) + two)
            here[part].append(jnp.where(inside, v[j] + one, 0.0))
        sums[part] = h
        squares[part] = g
    square_re, square_im = damping * damping - turning * turning, 2.0 * damping * turning
    first_re, first_im = 2.0 * damping - 4.0 * square_re, 2.0 * turning - 4.0 * square_im
    inner = [[here[part][j] + squares[part][j] - 4.0 * sums[part][j] for j in range(2)] for part in range(2)]
    spread = [[], []]
    for j in range(2):
        last = times(square_re, square_im, here, j)
        middle = times(first_re, first_im, here, j)
        edge = times(square_re, square_im, sums, j)
        core = times(square_re, square_im, inner, j)
        for part in range(2):
            third = behind(carry, (order, 2, part, j), edge[part])
            second = behind(carry, (order, 3, part, j), (wave[part][j] + core[part]) + third)
            whole = behind(carry, (order, 4, part, j), (middle[part] + edge[part]) + second)
            spread[part].append(last[part] + whole)
    return spread


def sweep_kernel(
    plan_ref, amp_hbm, phase_hbm, exit_ref, spr_ref, amp_ref, phase_ref, half, other, padded, windows, trans, inbox, spread_out, wave_out, waves, tall,
    amp_sem, phase_sem, half_sem, half_sent, exit_sem, trans_sem, in_sem, spr_sem, trans_sent, spr_sent, wave_sent,
):
    sec = lax.axis_index("sec")
    scan = lax.axis_index("scan")
    group = sec // G
    member = lax.rem(sec, G)
    groups = lax.axis_size("sec") // G
    top = group == groups - 1

    def at(g, m):
        return (g * G + m, scan)

    loads = (
        pltpu.make_async_copy(amp_hbm, amp_ref, amp_sem),
        pltpu.make_async_copy(phase_hbm, phase_ref, phase_sem),
    )
    for load in loads:
        load.start()
    barrier = pltpu.get_barrier_semaphore()
    for step in range(1, G):
        pl.semaphore_signal(barrier, 1, device_id=at(group, lax.rem(member + step, G)), device_id_type=MESH)

    partner = (sec, 1 - scan)
    pl.semaphore_signal(barrier, 1, device_id=partner, device_id_type=MESH)

    @pl.when(group > 0)
    def _():
        pl.semaphore_signal(barrier, 1, device_id=at(group - 1, member), device_id_type=MESH)

    @pl.when(jnp.logical_not(top))
    def _():
        pl.semaphore_signal(barrier, 1, device_id=at(group + 1, member), device_id_type=MESH)

    pl.semaphore_wait(barrier, G + jnp.where(group > 0, 1, 0) + jnp.where(top, 0, 1))
    mine = G - 1 - member
    delay = 2 * (mine + 1)
    exits = pltpu.make_async_copy(exit_ref.at[member], inbox.at[:, 0:W, :], exit_sem)

    @pl.when(top)
    def _():
        exits.start()

    def block_rows(block):
        return pl.ds(pl.multiple_of(block * BLOCK, BLOCK), BLOCK)

    def chunk(part, block):
        return pltpu.make_async_remote_copy(
            src_ref=half.at[part, block_rows(block), :],
            dst_ref=other.at[part, block_rows(block), :],
            send_sem=half_sent.at[part, block],
            recv_sem=half_sem.at[part, block],
            device_id=partner,
            device_id_type=MESH,
        )

    def place(part, block, value, owner):
        to = pl.ds(pl.multiple_of(TOP + owner * (OBJ // 2) + block * BLOCK, 8), BLOCK)
        for j in range(OBJ // 128):
            padded[part, j, to, :] = value[:, 128 * j : 128 * j + 128]

    for load in loads:
        load.wait()

    for part, wave in enumerate((jnp.cos, jnp.sin)):

        def make(block, unused):
            value = amp_ref[block_rows(block), :] * wave(phase_ref[block_rows(block), :]) * FIX
            value = jnp.where(value >= 0.0, value + 0.5, value - 0.5).astype(jnp.int32)
            half[part, block_rows(block), :] = value.astype(HELD)
            chunk(part, block).start()
            place(part, block, value, scan)
            return unused

        lax.fori_loop(0, BLOCKS, make, 0)
    waves[...] = jnp.zeros_like(waves)
    inbox[:, W:, :] = jnp.zeros((2, S * R - W, W), jnp.bfloat16)
    lane = lax.broadcasted_iota(jnp.int32, (R, 128), 1)

    def take(part):
        def some_rows(block, unused):
            chunk(part, block).wait()
            place(part, block, other[part, block_rows(block), :].astype(jnp.int32), 1 - scan)
            return unused

        lax.fori_loop(0, BLOCKS, some_rows, 0)

    def give(strip, parts):
        at_row = lax.broadcasted_iota(jnp.int32, (R, 128), 0) + (strip * R - delay)
        inside = jnp.logical_and(at_row >= 0, at_row < W)
        for part in parts:
            for position in range(G):
                keep = lane < 128 - plan_ref[position, 2]
                rows = pl.ds(plan_ref[position, 0] + (strip * R - delay + TOP), R)
                rolled = [
                    pltpu.roll(padded[part, plan_ref[position, 1] + j, rows, :], plan_ref[position, 3], 1) for j in range(3)
                ]
                for j in range(2):
                    value = jnp.where(inside, jnp.where(keep, rolled[j], rolled[j + 1]), 0)
                    windows[part, position, strip, :, 128 * j : 128 * j + 128] = value.astype(HELD)
            trans[part, strip, mine] = windows[part, member, strip]
            for step in range(1, G):
                person = lax.rem(member + step, G)
                pltpu.make_async_remote_copy(
                    src_ref=windows.at[part, person, strip],
                    dst_ref=trans.at[part, strip, mine],
                    send_sem=trans_sent,
                    recv_sem=trans_sem.at[part, strip],
                    device_id=at(group, person),
                    device_id_type=MESH,
                ).start()

    def gives(begin, end, parts):
        def some_strips(strip, unused):
            give(strip, parts)
            return unused

        lax.fori_loop(begin, end, some_strips, 0)

    take(0)
    gives(0, AHEAD, (0,))
    take(1)
    gives(0, AHEAD, (1,))
    gives(AHEAD, S, (0, 1))

    @pl.when(top)
    def _():
        exits.wait()

    row = lax.broadcasted_iota(jnp.int32, (R, 128), 0)

    def send_spread(strip, order):
        pltpu.make_async_remote_copy(
            src_ref=spread_out.at[strip, order],
            dst_ref=spr_ref.at[member, strip],
            send_sem=spr_sent,
            recv_sem=spr_sem,
            device_id=at(group, G - 1 - order),
            device_id_type=MESH,
        ).start()

    def one_strip(strip, unused):
        @pl.when(jnp.logical_and(strip < S - 1, jnp.logical_not(top)))
        def _():
            landed = inbox.at[:, pl.ds(pl.multiple_of(strip * R, R), R), :]
            pltpu.make_async_copy(landed, landed, in_sem.at[strip]).wait()

        for part in range(2):
            come = trans.at[part, strip, 0 : G - 1]
            pltpu.make_async_copy(come, come, trans_sem.at[part, strip]).wait()
        before = jnp.maximum(strip - 1, 0)
        at_strip = pl.multiple_of(strip * R, R)
        seen = pl.multiple_of(before * R, R)
        wave = [
            [inbox[part, pl.ds(at_strip, R), 128 * j : 128 * j + 128].astype(jnp.float32) for j in range(2)]
            for part in range(2)
        ]
        for order in range(G):
            at_row = row + (strip * R - 2 * order - 1)
            inside = jnp.logical_and(at_row >= 0, at_row < W)
            spread_re, spread_im = both_steps(waves, order, wave, inside, lane)
            wave = [[], []]
            for j in range(2):
                cols = slice(128 * j, 128 * j + 128)
                tall[order, 0, j, pl.ds(at_strip, R), :] = spread_re[j]
                tall[order, 1, j, pl.ds(at_strip, R), :] = spread_im[j]
                win_re = trans[0, strip, order, :, cols].astype(jnp.int32).astype(jnp.float32)
                win_im = trans[1, strip, order, :, cols].astype(jnp.int32).astype(jnp.float32)
                out_re = ((win_re * spread_re[j] + win_im * spread_im[j]) * (1.0 / FIX)).astype(jnp.bfloat16)
                out_im = ((win_re * spread_im[j] - win_im * spread_re[j]) * (1.0 / FIX)).astype(jnp.bfloat16)
                if order < G - 1:
                    wave[0].append(out_re.astype(jnp.float32))
                    wave[1].append(out_im.astype(jnp.float32))
                else:
                    wave_out[before, 0, :, cols] = out_re
                    wave_out[before, 1, :, cols] = out_im

        @pl.when(jnp.logical_and(strip > 0, group > 0))
        def _():
            pltpu.make_async_remote_copy(
                src_ref=wave_out.at[strip - 1],
                dst_ref=inbox.at[:, pl.ds(seen, R), :],
                send_sem=wave_sent,
                recv_sem=in_sem.at[strip - 1],
                device_id=at(group - 1, member),
                device_id_type=MESH,
            ).start()

        for order in range(G):
            lag = 2 * (order + 1)
            for part in range(2):
                for j in range(2):
                    spread_out[before, order, part, :, 128 * j : 128 * j + 128] = tall[
                        order, part, j, pl.ds(seen + lag, R), :
                    ].astype(jnp.bfloat16)

            @pl.when(jnp.logical_and(strip > 0, jnp.logical_and(group < LATE, member != G - 1 - order)))
            def _():
                send_spread(strip - 1, order)

        @pl.when(strip > 0)
        def _():
            spr_ref[member, strip - 1] = spread_out[strip - 1, mine]

        return unused

    lax.fori_loop(0, S, one_strip, 0)

    @pl.when(group >= LATE)
    def _():
        def rest(strip, unused):
            for order in range(G):

                @pl.when(member != G - 1 - order)
                def _():
                    send_spread(strip, order)

            return unused

        lax.fori_loop(0, S - 1, rest, 0)

    pltpu.make_async_copy(windows.at[:, 0 : G - 1], windows.at[:, 0 : G - 1], trans_sent).wait()
    pltpu.make_async_copy(spr_ref.at[0 : G - 1], spr_ref.at[0 : G - 1], spr_sent).wait()

    @pl.when(group > 0)
    def _():
        pltpu.make_async_copy(wave_out, wave_out, wave_sent).wait()

    pltpu.make_async_copy(spr_ref.at[0 : G - 1], spr_ref.at[0 : G - 1], spr_sem).wait()


def sweep(plan, amp, phase, exit_adjoint):
    return pl.pallas_call(
        sweep_kernel,
        out_shape=pltpu.VMEM((G, S - 1, 2, R, W), jnp.bfloat16),
        in_specs=[
            pl.BlockSpec(memory_space=pltpu.SMEM),
            pl.BlockSpec(memory_space=pl.ANY),
            pl.BlockSpec(memory_space=pl.ANY),
            pl.BlockSpec(memory_space=pl.ANY),
        ],
        out_specs=pl.BlockSpec(memory_space=pltpu.VMEM),
        scratch_shapes=[
            pltpu.VMEM((OBJ // 2, OBJ), jnp.float32),
            pltpu.VMEM((OBJ // 2, OBJ), jnp.float32),
            pltpu.VMEM((2, OBJ // 2, OBJ), HELD),
            pltpu.VMEM((2, OBJ // 2, OBJ), HELD),
            pltpu.VMEM((2, OBJ // 128 + 1, ROWS, 128), jnp.int32),
            pltpu.VMEM((2, G, S, R, W), HELD),
            pltpu.VMEM((2, S, G, R, W), HELD),
            pltpu.VMEM((2, S * R, W), jnp.bfloat16),
            pltpu.VMEM((S - 1, G, 2, R, W), jnp.bfloat16),
            pltpu.VMEM((S - 1, 2, R, W), jnp.bfloat16),
            pltpu.VMEM((G, 5, 2, 2, 8, 128), jnp.float32),
            pltpu.VMEM((G, 2, 2, S * R, 128), jnp.float32),
            pltpu.SemaphoreType.DMA,
            pltpu.SemaphoreType.DMA,
            pltpu.SemaphoreType.DMA((2, BLOCKS)),
            pltpu.SemaphoreType.DMA((2, BLOCKS)),
            pltpu.SemaphoreType.DMA,
            pltpu.SemaphoreType.DMA((2, S)),
            pltpu.SemaphoreType.DMA((S - 1,)),
            pltpu.SemaphoreType.DMA,
            pltpu.SemaphoreType.DMA,
            pltpu.SemaphoreType.DMA,
            pltpu.SemaphoreType.DMA,
        ],
        compiler_params=pltpu.CompilerParams(collective_id=0, has_side_effects=True, vmem_limit_bytes=62_390_272),
        name="sweep",
    )(plan, amp, phase, exit_adjoint)


def gather_kernel(other, offs_ref, fwd_ref, spr_ref, grad_ref, acc):
    scan = lax.axis_index("scan")
    start = ((1 - scan) if other else scan) * (OBJ // 2)
    acc[...] = jnp.zeros_like(acc)
    lane = lax.broadcasted_iota(jnp.int32, (RUN, 128), 1)

    def per_position(position, unused):
        row_at = offs_ref[position, 0]
        col_at = offs_ref[position, 1]
        column = col_at // 128
        over = lax.rem(col_at, 128)
        keep = lane >= over
        begin = jnp.maximum(start - row_at, 0) // RUN
        end = jnp.minimum((start + OBJ // 2 - row_at + RUN - 1) // RUN, W // RUN)

        def per_run(run, unused):
            rows = pl.ds(pl.multiple_of(run * RUN, RUN), RUN)
            to = pl.ds(row_at + run * RUN - start + RUN, RUN)
            terms = [[], []]
            for j in range(2):
                cols = slice(128 * j, 128 * j + 128)
                fwd_re = fwd_ref[position, 0, rows, cols].astype(jnp.float32)
                fwd_im = fwd_ref[position, 1, rows, cols].astype(jnp.float32)
                spread = [
                    jnp.concatenate([spr_ref[position, run * (RUN // R) + i, part, :, cols] for i in range(RUN // R)], axis=0)
                    for part in range(2)
                ]
                spread_re, spread_im = (part.astype(jnp.float32) for part in spread)
                terms[0].append(pltpu.roll(fwd_re * spread_re + fwd_im * spread_im, over, 1))
                terms[1].append(pltpu.roll(fwd_re * spread_im - fwd_im * spread_re, over, 1))
            for part in range(2):
                near, far = terms[part]
                acc[part, column, to, :] += jnp.where(keep, near, 0.0)
                acc[part, column + 1, to, :] += jnp.where(keep, far, near)
                acc[part, column + 2, to, :] += jnp.where(keep, 0.0, far)
            return unused

        lax.fori_loop(begin, end, per_run, 0)
        return unused

    lax.fori_loop(0, G, per_position, 0)

    def split(block, unused):
        rows = pl.ds(pl.multiple_of(block * BLOCK, BLOCK), BLOCK)
        source = pl.ds(pl.multiple_of(RUN + block * BLOCK, BLOCK), BLOCK)
        for part in range(2):
            for j in range(OBJ // 128):
                grad_ref[part, rows, 128 * j : 128 * j + 128] = acc[part, j, source, :].astype(grad_ref.dtype)
        return unused

    lax.fori_loop(0, BLOCKS, split, 0)


def gather(offsets, forward, spread, other):
    return pl.pallas_call(
        functools.partial(gather_kernel, other),
        out_shape=jax.ShapeDtypeStruct((2, OBJ // 2, OBJ), jnp.bfloat16 if other else jnp.float32),
        in_specs=[
            pl.BlockSpec(memory_space=pltpu.SMEM),
            pl.BlockSpec(memory_space=pltpu.VMEM),
            pl.BlockSpec(memory_space=pltpu.VMEM),
        ],
        out_specs=pl.BlockSpec(memory_space=pltpu.VMEM),
        scratch_shapes=[pltpu.VMEM((2, OBJ // 128 + 1, OBJ // 2 + 2 * RUN, 128), jnp.float32)],
        compiler_params=pltpu.CompilerParams(vmem_limit_bytes=16 << 20),
        cost_estimate=pl.CostEstimate(flops=20_000_000, bytes_accessed=6_000_000, transcendentals=0),
        name="gather_other" if other else "gather_own",
    )(offsets, forward, spread)


def on_device(obj_amp, obj_phase, forward_waves, exit_adjoint, offsets):
    column, over = offsets[:, 1] // 128, offsets[:, 1] % 128
    plan = jnp.stack([offsets[:, 0], column, over, (128 - over) % 128], axis=1)
    spread = sweep(plan, obj_amp[0], obj_phase[0], exit_adjoint)
    spread = pltpu.with_memory_space_constraint(spread, pltpu.VMEM)
    forward = pltpu.with_memory_space_constraint(forward_waves[0], pltpu.VMEM)
    leave = gather(offsets, forward, spread, True)
    come = lax.ppermute(leave, "scan", [(0, 1), (1, 0)])
    keep = gather(offsets, forward, spread, False)
    return (keep + come.astype(jnp.float32))[None]


def solution(mesh):
    in_specs = (
        P("sec", "scan", None),
        P("sec", "scan", None),
        P("sec", "scan", None, None, None),
        P("scan", None, None, None),
        P("scan", None),
    )
    out_specs = P("sec", None, "scan", None)
    return jax.shard_map(
        on_device, mesh=mesh, in_specs=in_specs, out_specs=out_specs, check_vma=False
    )
```

```python
import functools

import jax
import jax.numpy as jnp
from jax import lax
from jax.experimental import pallas as pl
from jax.experimental.pallas import tpu as pltpu
from jax.sharding import PartitionSpec as P

MESH = pl.DeviceIdType.MESH

damping = 0.0005
turning = 0.011

G = 8
R = 16
SKEW = 2 * G
W = 256
OBJ = 512
S = (W + SKEW) // R
TOP = 16
ROWS = OBJ + 40
AHEAD = 7
LATE = 5
COLS = OBJ + 128
FIX = 32767.0
HELD = jnp.int16
RUN = 64
BLOCK = 32
BLOCKS = OBJ // 2 // BLOCK


def behind(carry, at, value):
    top = lax.broadcasted_iota(jnp.int32, (8, 128), 0) < 1
    pieces = [carry[at]] + [value[8 * i : 8 * i + 8] for i in range(R // 8)]
    carry[at] = pieces[-1]
    rolled = [pltpu.roll(piece, 1, 0) for piece in pieces]
    return jnp.concatenate([jnp.where(top, rolled[i], rolled[i + 1]) for i in range(R // 8)], axis=0)


def times(re, im, value, j):
    return re * value[0][j] + im * value[1][j], re * value[1][j] - im * value[0][j]


def both_steps(carry, order, wave, inside, lane):
    sums, squares, here = [[], []], [[], []], [[], []]
    for part in range(2):
        v = wave[part]
        left1, left2 = ([pltpu.roll(v[j], n, 1) for j in range(2)] for n in (1, 2))
        right1, right2 = ([pltpu.roll(v[j], 128 - n, 1) for j in range(2)] for n in (1, 2))

        def pair(left, right, n):
            low, high = lane < n, lane >= 128 - n
            return [
                jnp.where(low, 0.0, left[0]) + jnp.where(high, right[1], right[0]),
                jnp.where(low, left[0], left[1]) + jnp.where(high, 0.0, right[1]),
            ]

        h = pair(left1, right1, 1)
        g = pair(left2, right2, 2)
        own = [jnp.where(lane == 0, 1.0, 2.0), jnp.where(lane == 127, 1.0, 2.0)]
        for j in range(2):
            g[j] = g[j] + own[j] * v[j]
            two = behind(carry, (order, 0, part, j), v[j])
            one = behind(carry, (order, 1, part, j), (h[j] - 4.0 * v[j]) + two)
            here[part].append(jnp.where(inside, v[j] + one, 0.0))
        sums[part] = h
        squares[part] = g
    square_re, square_im = damping * damping - turning * turning, 2.0 * damping * turning
    first_re, first_im = 2.0 * damping - 4.0 * square_re, 2.0 * turning - 4.0 * square_im
    inner = [[here[part][j] + squares[part][j] - 4.0 * sums[part][j] for j in range(2)] for part in range(2)]
    spread = [[], []]
    for j in range(2):
        last = times(square_re, square_im, here, j)
        middle = times(first_re, first_im, here, j)
        edge = times(square_re, square_im, sums, j)
        core = times(square_re, square_im, inner, j)
        for part in range(2):
            third = behind(carry, (order, 2, part, j), edge[part])
            second = behind(carry, (order, 3, part, j), (wave[part][j] + core[part]) + third)
            whole = behind(carry, (order, 4, part, j), (middle[part] + edge[part]) + second)
            spread[part].append(last[part] + whole)
    return spread


def sweep_kernel(
    offs_ref, amp_hbm, phase_hbm, exit_ref, spr_ref, amp_ref, phase_ref, half, other, padded, windows, trans, inbox, spread_out, wave_out, waves, tall,
    amp_sem, phase_sem, half_sem, half_sent, exit_sem, trans_sem, in_sem, spr_sem, trans_sent, spr_sent, wave_sent,
):
    sec = lax.axis_index("sec")
    scan = lax.axis_index("scan")
    group = sec // G
    member = lax.rem(sec, G)
    groups = lax.axis_size("sec") // G
    top = group == groups - 1

    def at(g, m):
        return (g * G + m, scan)

    loads = (
        pltpu.make_async_copy(amp_hbm, amp_ref, amp_sem),
        pltpu.make_async_copy(phase_hbm, phase_ref, phase_sem),
    )
    for load in loads:
        load.start()
    barrier = pltpu.get_barrier_semaphore()
    for step in range(1, G):
        pl.semaphore_signal(barrier, 1, device_id=at(group, lax.rem(member + step, G)), device_id_type=MESH)

    partner = (sec, 1 - scan)
    pl.semaphore_signal(barrier, 1, device_id=partner, device_id_type=MESH)

    @pl.when(group > 0)
    def _():
        pl.semaphore_signal(barrier, 1, device_id=at(group - 1, member), device_id_type=MESH)

    @pl.when(jnp.logical_not(top))
    def _():
        pl.semaphore_signal(barrier, 1, device_id=at(group + 1, member), device_id_type=MESH)

    pl.semaphore_wait(barrier, G + jnp.where(group > 0, 1, 0) + jnp.where(top, 0, 1))
    mine = G - 1 - member
    delay = 2 * (mine + 1)
    exits = pltpu.make_async_copy(exit_ref.at[member], inbox.at[:, 0:W, :], exit_sem)

    @pl.when(top)
    def _():
        exits.start()

    def block_rows(block):
        return pl.ds(pl.multiple_of(block * BLOCK, BLOCK), BLOCK)

    def chunk(part, block):
        return pltpu.make_async_remote_copy(
            src_ref=half.at[part, block_rows(block), :],
            dst_ref=other.at[part, block_rows(block), :],
            send_sem=half_sent.at[part, block],
            recv_sem=half_sem.at[part, block],
            device_id=partner,
            device_id_type=MESH,
        )

    def place(part, block, value, owner):
        to = pl.ds(pl.multiple_of(TOP + owner * (OBJ // 2) + block * BLOCK, 8), BLOCK)
        for j in range(OBJ // 128):
            padded[part, j, to, :] = value[:, 128 * j : 128 * j + 128]

    for load in loads:
        load.wait()

    for part, wave in enumerate((jnp.cos, jnp.sin)):

        def make(block, unused):
            value = amp_ref[block_rows(block), :] * wave(phase_ref[block_rows(block), :]) * FIX
            value = jnp.where(value >= 0.0, value + 0.5, value - 0.5).astype(jnp.int32)
            half[part, block_rows(block), :] = value.astype(HELD)
            chunk(part, block).start()
            place(part, block, value, scan)
            return unused

        lax.fori_loop(0, BLOCKS, make, 0)
    waves[...] = jnp.zeros_like(waves)
    inbox[:, W:, :] = jnp.zeros((2, S * R - W, W), jnp.bfloat16)
    lane = lax.broadcasted_iota(jnp.int32, (R, 128), 1)

    def take(part):
        def some_rows(block, unused):
            chunk(part, block).wait()
            place(part, block, other[part, block_rows(block), :].astype(jnp.int32), 1 - scan)
            return unused

        lax.fori_loop(0, BLOCKS, some_rows, 0)

    def give(strip, parts):
        at_row = lax.broadcasted_iota(jnp.int32, (R, 128), 0) + (strip * R - delay)
        inside = jnp.logical_and(at_row >= 0, at_row < W)
        for part in parts:
            for position in range(G):
                column = lax.shift_right_logical(offs_ref[position, 1], 7)
                over = lax.bitwise_and(offs_ref[position, 1], 127)
                turn = lax.bitwise_and(128 - over, 127)
                keep = lane < 128 - over
                rows = pl.ds(offs_ref[position, 0] + (strip * R - delay + TOP), R)
                rolled = [pltpu.roll(padded[part, column + j, rows, :], turn, 1) for j in range(3)]
                for j in range(2):
                    value = jnp.where(inside, jnp.where(keep, rolled[j], rolled[j + 1]), 0)
                    windows[part, position, strip, :, 128 * j : 128 * j + 128] = value.astype(HELD)
            trans[part, strip, mine] = windows[part, member, strip]
            for step in range(1, G):
                person = lax.rem(member + step, G)
                pltpu.make_async_remote_copy(
                    src_ref=windows.at[part, person, strip],
                    dst_ref=trans.at[part, strip, mine],
                    send_sem=trans_sent,
                    recv_sem=trans_sem.at[part, strip],
                    device_id=at(group, person),
                    device_id_type=MESH,
                ).start()

    def gives(begin, end, parts):
        def some_strips(strip, unused):
            give(strip, parts)
            return unused

        lax.fori_loop(begin, end, some_strips, 0)

    take(0)
    gives(0, AHEAD, (0,))
    take(1)
    gives(0, AHEAD, (1,))
    gives(AHEAD, S, (0, 1))

    @pl.when(top)
    def _():
        exits.wait()

    row = lax.broadcasted_iota(jnp.int32, (R, 128), 0)

    def send_spread(strip, order):
        pltpu.make_async_remote_copy(
            src_ref=spread_out.at[strip, order],
            dst_ref=spr_ref.at[member, strip],
            send_sem=spr_sent,
            recv_sem=spr_sem,
            device_id=at(group, G - 1 - order),
            device_id_type=MESH,
        ).start()

    def one_strip(strip, unused):
        @pl.when(jnp.logical_and(strip < S - 1, jnp.logical_not(top)))
        def _():
            landed = inbox.at[:, pl.ds(pl.multiple_of(strip * R, R), R), :]
            pltpu.make_async_copy(landed, landed, in_sem.at[strip]).wait()

        for part in range(2):
            come = trans.at[part, strip, 0 : G - 1]
            pltpu.make_async_copy(come, come, trans_sem.at[part, strip]).wait()
        before = jnp.maximum(strip - 1, 0)
        at_strip = pl.multiple_of(strip * R, R)
        seen = pl.multiple_of(before * R, R)
        wave = [
            [inbox[part, pl.ds(at_strip, R), 128 * j : 128 * j + 128].astype(jnp.float32) for j in range(2)]
            for part in range(2)
        ]
        for order in range(G):
            at_row = row + (strip * R - 2 * order - 1)
            inside = jnp.logical_and(at_row >= 0, at_row < W)
            spread_re, spread_im = both_steps(waves, order, wave, inside, lane)
            wave = [[], []]
            for j in range(2):
                cols = slice(128 * j, 128 * j + 128)
                tall[order, 0, j, pl.ds(at_strip, R), :] = spread_re[j]
                tall[order, 1, j, pl.ds(at_strip, R), :] = spread_im[j]
                win_re = trans[0, strip, order, :, cols].astype(jnp.int32).astype(jnp.float32)
                win_im = trans[1, strip, order, :, cols].astype(jnp.int32).astype(jnp.float32)
                out_re = ((win_re * spread_re[j] + win_im * spread_im[j]) * (1.0 / FIX)).astype(jnp.bfloat16)
                out_im = ((win_re * spread_im[j] - win_im * spread_re[j]) * (1.0 / FIX)).astype(jnp.bfloat16)
                if order < G - 1:
                    wave[0].append(out_re.astype(jnp.float32))
                    wave[1].append(out_im.astype(jnp.float32))
                else:
                    wave_out[before, 0, :, cols] = out_re
                    wave_out[before, 1, :, cols] = out_im

        @pl.when(jnp.logical_and(strip > 0, group > 0))
        def _():
            pltpu.make_async_remote_copy(
                src_ref=wave_out.at[strip - 1],
                dst_ref=inbox.at[:, pl.ds(seen, R), :],
                send_sem=wave_sent,
                recv_sem=in_sem.at[strip - 1],
                device_id=at(group - 1, member),
                device_id_type=MESH,
            ).start()

        for order in range(G):
            lag = 2 * (order + 1)
            for part in range(2):
                for j in range(2):
                    spread_out[before, order, part, :, 128 * j : 128 * j + 128] = tall[
                        order, part, j, pl.ds(seen + lag, R), :
                    ].astype(jnp.bfloat16)

            @pl.when(jnp.logical_and(strip > 0, jnp.logical_and(group < LATE, member != G - 1 - order)))
            def _():
                send_spread(strip - 1, order)

        @pl.when(strip > 0)
        def _():
            spr_ref[member, strip - 1] = spread_out[strip - 1, mine]

        return unused

    lax.fori_loop(0, S, one_strip, 0)

    @pl.when(group >= LATE)
    def _():
        def rest(strip, unused):
            for order in range(G):

                @pl.when(member != G - 1 - order)
                def _():
                    send_spread(strip, order)

            return unused

        lax.fori_loop(0, S - 1, rest, 0)

    pltpu.make_async_copy(windows.at[:, 0 : G - 1], windows.at[:, 0 : G - 1], trans_sent).wait()
    pltpu.make_async_copy(spr_ref.at[0 : G - 1], spr_ref.at[0 : G - 1], spr_sent).wait()

    @pl.when(group > 0)
    def _():
        pltpu.make_async_copy(wave_out, wave_out, wave_sent).wait()

    pltpu.make_async_copy(spr_ref.at[0 : G - 1], spr_ref.at[0 : G - 1], spr_sem).wait()


def sweep(offsets, amp, phase, exit_adjoint):
    return pl.pallas_call(
        sweep_kernel,
        out_shape=pltpu.VMEM((G, S - 1, 2, R, W), jnp.bfloat16),
        in_specs=[
            pl.BlockSpec(memory_space=pltpu.SMEM),
            pl.BlockSpec(memory_space=pl.ANY),
            pl.BlockSpec(memory_space=pl.ANY),
            pl.BlockSpec(memory_space=pl.ANY),
        ],
        out_specs=pl.BlockSpec(memory_space=pltpu.VMEM),
        scratch_shapes=[
            pltpu.VMEM((OBJ // 2, OBJ), jnp.float32),
            pltpu.VMEM((OBJ // 2, OBJ), jnp.float32),
            pltpu.VMEM((2, OBJ // 2, OBJ), HELD),
            pltpu.VMEM((2, OBJ // 2, OBJ), HELD),
            pltpu.VMEM((2, OBJ // 128 + 1, ROWS, 128), jnp.int32),
            pltpu.VMEM((2, G, S, R, W), HELD),
            pltpu.VMEM((2, S, G, R, W), HELD),
            pltpu.VMEM((2, S * R, W), jnp.bfloat16),
            pltpu.VMEM((S - 1, G, 2, R, W), jnp.bfloat16),
            pltpu.VMEM((S - 1, 2, R, W), jnp.bfloat16),
            pltpu.VMEM((G, 5, 2, 2, 8, 128), jnp.float32),
            pltpu.VMEM((G, 2, 2, S * R, 128), jnp.float32),
            pltpu.SemaphoreType.DMA,
            pltpu.SemaphoreType.DMA,
            pltpu.SemaphoreType.DMA((2, BLOCKS)),
            pltpu.SemaphoreType.DMA((2, BLOCKS)),
            pltpu.SemaphoreType.DMA,
            pltpu.SemaphoreType.DMA((2, S)),
            pltpu.SemaphoreType.DMA((S - 1,)),
            pltpu.SemaphoreType.DMA,
            pltpu.SemaphoreType.DMA,
            pltpu.SemaphoreType.DMA,
            pltpu.SemaphoreType.DMA,
        ],
        compiler_params=pltpu.CompilerParams(collective_id=0, has_side_effects=True, vmem_limit_bytes=62_390_272),
        name="sweep",
    )(offsets, amp, phase, exit_adjoint)


def gather_kernel(other, offs_ref, fwd_ref, spr_ref, grad_ref, acc):
    scan = lax.axis_index("scan")
    start = ((1 - scan) if other else scan) * (OBJ // 2)
    acc[...] = jnp.zeros_like(acc)
    lane = lax.broadcasted_iota(jnp.int32, (RUN, 128), 1)

    def per_position(position, unused):
        row_at = offs_ref[position, 0]
        col_at = offs_ref[position, 1]
        column = col_at // 128
        over = lax.rem(col_at, 128)
        keep = lane >= over
        begin = jnp.maximum(start - row_at, 0) // RUN
        end = jnp.minimum((start + OBJ // 2 - row_at + RUN - 1) // RUN, W // RUN)

        def per_run(run, unused):
            rows = pl.ds(pl.multiple_of(run * RUN, RUN), RUN)
            to = pl.ds(row_at + run * RUN - start + RUN, RUN)
            terms = [[], []]
            for j in range(2):
                cols = slice(128 * j, 128 * j + 128)
                fwd_re = fwd_ref[position, 0, rows, cols].astype(jnp.float32)
                fwd_im = fwd_ref[position, 1, rows, cols].astype(jnp.float32)
                spread = [
                    jnp.concatenate([spr_ref[position, run * (RUN // R) + i, part, :, cols] for i in range(RUN // R)], axis=0)
                    for part in range(2)
                ]
                spread_re, spread_im = (part.astype(jnp.float32) for part in spread)
                terms[0].append(pltpu.roll(fwd_re * spread_re + fwd_im * spread_im, over, 1))
                terms[1].append(pltpu.roll(fwd_re * spread_im - fwd_im * spread_re, over, 1))
            for part in range(2):
                near, far = terms[part]
                acc[part, column, to, :] += jnp.where(keep, near, 0.0)
                acc[part, column + 1, to, :] += jnp.where(keep, far, near)
                acc[part, column + 2, to, :] += jnp.where(keep, 0.0, far)
            return unused

        lax.fori_loop(begin, end, per_run, 0)
        return unused

    lax.fori_loop(0, G, per_position, 0)

    def split(block, unused):
        rows = pl.ds(pl.multiple_of(block * BLOCK, BLOCK), BLOCK)
        source = pl.ds(pl.multiple_of(RUN + block * BLOCK, BLOCK), BLOCK)
        for part in range(2):
            for j in range(OBJ // 128):
                grad_ref[part, rows, 128 * j : 128 * j + 128] = acc[part, j, source, :].astype(grad_ref.dtype)
        return unused

    lax.fori_loop(0, BLOCKS, split, 0)


def gather(offsets, forward, spread, other):
    return pl.pallas_call(
        functools.partial(gather_kernel, other),
        out_shape=jax.ShapeDtypeStruct((2, OBJ // 2, OBJ), jnp.bfloat16 if other else jnp.float32),
        in_specs=[
            pl.BlockSpec(memory_space=pltpu.SMEM),
            pl.BlockSpec(memory_space=pltpu.VMEM),
            pl.BlockSpec(memory_space=pltpu.VMEM),
        ],
        out_specs=pl.BlockSpec(memory_space=pltpu.VMEM),
        scratch_shapes=[pltpu.VMEM((2, OBJ // 128 + 1, OBJ // 2 + 2 * RUN, 128), jnp.float32)],
        compiler_params=pltpu.CompilerParams(vmem_limit_bytes=16 << 20),
        cost_estimate=pl.CostEstimate(flops=20_000_000, bytes_accessed=6_000_000, transcendentals=0),
        name="gather_other" if other else "gather_own",
    )(offsets, forward, spread)


def on_device(obj_amp, obj_phase, forward_waves, exit_adjoint, offsets):
    spread = sweep(offsets, obj_amp[0], obj_phase[0], exit_adjoint)
    spread = pltpu.with_memory_space_constraint(spread, pltpu.VMEM)
    forward = pltpu.with_memory_space_constraint(forward_waves[0], pltpu.VMEM)
    leave = gather(offsets, forward, spread, True)
    come = lax.ppermute(leave, "scan", [(0, 1), (1, 0)])
    keep = gather(offsets, forward, spread, False)
    return (keep + come.astype(jnp.float32))[None]


def solution(mesh):
    in_specs = (
        P("sec", "scan", None),
        P("sec", "scan", None),
        P("sec", "scan", None, None, None),
        P("scan", None, None, None),
        P("scan", None),
    )
    out_specs = P("sec", None, "scan", None)
    return jax.shard_map(
        on_device, mesh=mesh, in_specs=in_specs, out_specs=out_specs, check_vma=False
    )
```

```python
import functools

import jax
import jax.numpy as jnp
from jax import lax
from jax.experimental import pallas as pl
from jax.experimental.pallas import tpu as pltpu
from jax.sharding import PartitionSpec as P

MESH = pl.DeviceIdType.MESH

damping = 0.0005
turning = 0.011

G = 8
R = 16
SKEW = 2 * G
W = 256
OBJ = 512
S = (W + SKEW) // R
TOP = 16
ROWS = OBJ + 40
AHEAD = 7
LATE = 5
COLS = OBJ + 128
FIX = 32767.0
HELD = jnp.int16
RUN = 128
BLOCK = 32
BLOCKS = OBJ // 2 // BLOCK


def behind(carry, at, value):
    top = lax.broadcasted_iota(jnp.int32, (8, 128), 0) < 1
    pieces = [carry[at]] + [value[8 * i : 8 * i + 8] for i in range(R // 8)]
    carry[at] = pieces[-1]
    rolled = [pltpu.roll(piece, 1, 0) for piece in pieces]
    return jnp.concatenate([jnp.where(top, rolled[i], rolled[i + 1]) for i in range(R // 8)], axis=0)


def times(re, im, value, j):
    return re * value[0][j] + im * value[1][j], re * value[1][j] - im * value[0][j]


def both_steps(carry, order, wave, inside, lane):
    sums, squares, here = [[], []], [[], []], [[], []]
    for part in range(2):
        v = wave[part]
        left1, left2 = ([pltpu.roll(v[j], n, 1) for j in range(2)] for n in (1, 2))
        right1, right2 = ([pltpu.roll(v[j], 128 - n, 1) for j in range(2)] for n in (1, 2))

        def pair(left, right, n):
            low, high = lane < n, lane >= 128 - n
            return [
                jnp.where(low, 0.0, left[0]) + jnp.where(high, right[1], right[0]),
                jnp.where(low, left[0], left[1]) + jnp.where(high, 0.0, right[1]),
            ]

        h = pair(left1, right1, 1)
        g = pair(left2, right2, 2)
        own = [jnp.where(lane == 0, 1.0, 2.0), jnp.where(lane == 127, 1.0, 2.0)]
        for j in range(2):
            g[j] = g[j] + own[j] * v[j]
            two = behind(carry, (order, 0, part, j), v[j])
            one = behind(carry, (order, 1, part, j), (h[j] - 4.0 * v[j]) + two)
            here[part].append(jnp.where(inside, v[j] + one, 0.0))
        sums[part] = h
        squares[part] = g
    square_re, square_im = damping * damping - turning * turning, 2.0 * damping * turning
    first_re, first_im = 2.0 * damping - 4.0 * square_re, 2.0 * turning - 4.0 * square_im
    inner = [[here[part][j] + squares[part][j] - 4.0 * sums[part][j] for j in range(2)] for part in range(2)]
    spread = [[], []]
    for j in range(2):
        last = times(square_re, square_im, here, j)
        middle = times(first_re, first_im, here, j)
        edge = times(square_re, square_im, sums, j)
        core = times(square_re, square_im, inner, j)
        for part in range(2):
            third = behind(carry, (order, 2, part, j), edge[part])
            second = behind(carry, (order, 3, part, j), (wave[part][j] + core[part]) + third)
            whole = behind(carry, (order, 4, part, j), (middle[part] + edge[part]) + second)
            spread[part].append(last[part] + whole)
    return spread


def sweep_kernel(
    offs_ref, amp_hbm, phase_hbm, exit_ref, spr_ref, amp_ref, phase_ref, half, other, padded, windows, trans, inbox, spread_out, wave_out, waves, tall,
    amp_sem, phase_sem, half_sem, half_sent, exit_sem, trans_sem, in_sem, spr_sem, trans_sent, spr_sent, wave_sent,
):
    sec = lax.axis_index("sec")
    scan = lax.axis_index("scan")
    group = sec // G
    member = lax.rem(sec, G)
    groups = lax.axis_size("sec") // G
    top = group == groups - 1

    def at(g, m):
        return (g * G + m, scan)

    loads = (
        pltpu.make_async_copy(amp_hbm, amp_ref, amp_sem),
        pltpu.make_async_copy(phase_hbm, phase_ref, phase_sem),
    )
    for load in loads:
        load.start()
    barrier = pltpu.get_barrier_semaphore()
    for step in range(1, G):
        pl.semaphore_signal(barrier, 1, device_id=at(group, lax.rem(member + step, G)), device_id_type=MESH)

    partner = (sec, 1 - scan)
    pl.semaphore_signal(barrier, 1, device_id=partner, device_id_type=MESH)

    @pl.when(group > 0)
    def _():
        pl.semaphore_signal(barrier, 1, device_id=at(group - 1, member), device_id_type=MESH)

    @pl.when(jnp.logical_not(top))
    def _():
        pl.semaphore_signal(barrier, 1, device_id=at(group + 1, member), device_id_type=MESH)

    pl.semaphore_wait(barrier, G + jnp.where(group > 0, 1, 0) + jnp.where(top, 0, 1))
    mine = G - 1 - member
    delay = 2 * (mine + 1)
    exits = pltpu.make_async_copy(exit_ref.at[member], inbox.at[:, 0:W, :], exit_sem)

    @pl.when(top)
    def _():
        exits.start()

    def block_rows(block):
        return pl.ds(pl.multiple_of(block * BLOCK, BLOCK), BLOCK)

    def chunk(part, block):
        return pltpu.make_async_remote_copy(
            src_ref=half.at[part, block_rows(block), :],
            dst_ref=other.at[part, block_rows(block), :],
            send_sem=half_sent.at[part, block],
            recv_sem=half_sem.at[part, block],
            device_id=partner,
            device_id_type=MESH,
        )

    def place(part, block, value, owner):
        to = pl.ds(pl.multiple_of(TOP + owner * (OBJ // 2) + block * BLOCK, 8), BLOCK)
        for j in range(OBJ // 128):
            padded[part, j, to, :] = value[:, 128 * j : 128 * j + 128]

    for load in loads:
        load.wait()

    for part, wave in enumerate((jnp.cos, jnp.sin)):

        def make(block, unused):
            value = amp_ref[block_rows(block), :] * wave(phase_ref[block_rows(block), :]) * FIX
            value = jnp.where(value >= 0.0, value + 0.5, value - 0.5).astype(jnp.int32)
            half[part, block_rows(block), :] = value.astype(HELD)
            chunk(part, block).start()
            place(part, block, value, scan)
            return unused

        lax.fori_loop(0, BLOCKS, make, 0)
    waves[...] = jnp.zeros_like(waves)
    inbox[:, W:, :] = jnp.zeros((2, S * R - W, W), jnp.bfloat16)
    lane = lax.broadcasted_iota(jnp.int32, (R, 128), 1)

    def take(part):
        def some_rows(block, unused):
            chunk(part, block).wait()
            place(part, block, other[part, block_rows(block), :].astype(jnp.int32), 1 - scan)
            return unused

        lax.fori_loop(0, BLOCKS, some_rows, 0)

    def give(strip, parts):
        at_row = lax.broadcasted_iota(jnp.int32, (R, 128), 0) + (strip * R - delay)
        inside = jnp.logical_and(at_row >= 0, at_row < W)
        for part in parts:
            for position in range(G):
                column = lax.shift_right_logical(offs_ref[position, 1], 7)
                over = lax.bitwise_and(offs_ref[position, 1], 127)
                turn = lax.bitwise_and(128 - over, 127)
                keep = lane < 128 - over
                rows = pl.ds(offs_ref[position, 0] + (strip * R - delay + TOP), R)
                rolled = [pltpu.roll(padded[part, column + j, rows, :], turn, 1) for j in range(3)]
                for j in range(2):
                    value = jnp.where(inside, jnp.where(keep, rolled[j], rolled[j + 1]), 0)
                    windows[part, position, strip, :, 128 * j : 128 * j + 128] = value.astype(HELD)
            trans[part, strip, mine] = windows[part, member, strip]
            for step in range(1, G):
                person = lax.rem(member + step, G)
                pltpu.make_async_remote_copy(
                    src_ref=windows.at[part, person, strip],
                    dst_ref=trans.at[part, strip, mine],
                    send_sem=trans_sent,
                    recv_sem=trans_sem.at[part, strip],
                    device_id=at(group, person),
                    device_id_type=MESH,
                ).start()

    def gives(begin, end, parts):
        def some_strips(strip, unused):
            give(strip, parts)
            return unused

        lax.fori_loop(begin, end, some_strips, 0)

    take(0)
    gives(0, AHEAD, (0,))
    take(1)
    gives(0, AHEAD, (1,))
    gives(AHEAD, S, (0, 1))

    @pl.when(top)
    def _():
        exits.wait()

    row = lax.broadcasted_iota(jnp.int32, (R, 128), 0)

    def send_spread(strip, order):
        pltpu.make_async_remote_copy(
            src_ref=spread_out.at[strip, order],
            dst_ref=spr_ref.at[member, strip],
            send_sem=spr_sent,
            recv_sem=spr_sem,
            device_id=at(group, G - 1 - order),
            device_id_type=MESH,
        ).start()

    def one_strip(strip, unused):
        @pl.when(jnp.logical_and(strip < S - 1, jnp.logical_not(top)))
        def _():
            landed = inbox.at[:, pl.ds(pl.multiple_of(strip * R, R), R), :]
            pltpu.make_async_copy(landed, landed, in_sem.at[strip]).wait()

        for part in range(2):
            come = trans.at[part, strip, 0 : G - 1]
            pltpu.make_async_copy(come, come, trans_sem.at[part, strip]).wait()
        before = jnp.maximum(strip - 1, 0)
        at_strip = pl.multiple_of(strip * R, R)
        seen = pl.multiple_of(before * R, R)
        wave = [
            [inbox[part, pl.ds(at_strip, R), 128 * j : 128 * j + 128].astype(jnp.float32) for j in range(2)]
            for part in range(2)
        ]
        for order in range(G):
            at_row = row + (strip * R - 2 * order - 1)
            inside = jnp.logical_and(at_row >= 0, at_row < W)
            spread_re, spread_im = both_steps(waves, order, wave, inside, lane)
            wave = [[], []]
            for j in range(2):
                cols = slice(128 * j, 128 * j + 128)
                tall[order, 0, j, pl.ds(at_strip, R), :] = spread_re[j]
                tall[order, 1, j, pl.ds(at_strip, R), :] = spread_im[j]
                win_re = trans[0, strip, order, :, cols].astype(jnp.int32).astype(jnp.float32)
                win_im = trans[1, strip, order, :, cols].astype(jnp.int32).astype(jnp.float32)
                out_re = ((win_re * spread_re[j] + win_im * spread_im[j]) * (1.0 / FIX)).astype(jnp.bfloat16)
                out_im = ((win_re * spread_im[j] - win_im * spread_re[j]) * (1.0 / FIX)).astype(jnp.bfloat16)
                if order < G - 1:
                    wave[0].append(out_re.astype(jnp.float32))
                    wave[1].append(out_im.astype(jnp.float32))
                else:
                    wave_out[before, 0, :, cols] = out_re
                    wave_out[before, 1, :, cols] = out_im

        @pl.when(jnp.logical_and(strip > 0, group > 0))
        def _():
            pltpu.make_async_remote_copy(
                src_ref=wave_out.at[strip - 1],
                dst_ref=inbox.at[:, pl.ds(seen, R), :],
                send_sem=wave_sent,
                recv_sem=in_sem.at[strip - 1],
                device_id=at(group - 1, member),
                device_id_type=MESH,
            ).start()

        for order in range(G):
            lag = 2 * (order + 1)
            for part in range(2):
                for j in range(2):
                    spread_out[before, order, part, :, 128 * j : 128 * j + 128] = tall[
                        order, part, j, pl.ds(seen + lag, R), :
                    ].astype(jnp.bfloat16)

            @pl.when(jnp.logical_and(strip > 0, jnp.logical_and(group < LATE, member != G - 1 - order)))
            def _():
                send_spread(strip - 1, order)

        @pl.when(strip > 0)
        def _():
            spr_ref[member, strip - 1] = spread_out[strip - 1, mine]

        return unused

    lax.fori_loop(0, S, one_strip, 0)

    @pl.when(group >= LATE)
    def _():
        def rest(strip, unused):
            for order in range(G):

                @pl.when(member != G - 1 - order)
                def _():
                    send_spread(strip, order)

            return unused

        lax.fori_loop(0, S - 1, rest, 0)

    pltpu.make_async_copy(windows.at[:, 0 : G - 1], windows.at[:, 0 : G - 1], trans_sent).wait()
    pltpu.make_async_copy(spr_ref.at[0 : G - 1], spr_ref.at[0 : G - 1], spr_sent).wait()

    @pl.when(group > 0)
    def _():
        pltpu.make_async_copy(wave_out, wave_out, wave_sent).wait()

    pltpu.make_async_copy(spr_ref.at[0 : G - 1], spr_ref.at[0 : G - 1], spr_sem).wait()


def sweep(offsets, amp, phase, exit_adjoint):
    return pl.pallas_call(
        sweep_kernel,
        out_shape=pltpu.VMEM((G, S - 1, 2, R, W), jnp.bfloat16),
        in_specs=[
            pl.BlockSpec(memory_space=pltpu.SMEM),
            pl.BlockSpec(memory_space=pl.ANY),
            pl.BlockSpec(memory_space=pl.ANY),
            pl.BlockSpec(memory_space=pl.ANY),
        ],
        out_specs=pl.BlockSpec(memory_space=pltpu.VMEM),
        scratch_shapes=[
            pltpu.VMEM((OBJ // 2, OBJ), jnp.float32),
            pltpu.VMEM((OBJ // 2, OBJ), jnp.float32),
            pltpu.VMEM((2, OBJ // 2, OBJ), HELD),
            pltpu.VMEM((2, OBJ // 2, OBJ), HELD),
            pltpu.VMEM((2, OBJ // 128 + 1, ROWS, 128), jnp.int32),
            pltpu.VMEM((2, G, S, R, W), HELD),
            pltpu.VMEM((2, S, G, R, W), HELD),
            pltpu.VMEM((2, S * R, W), jnp.bfloat16),
            pltpu.VMEM((S - 1, G, 2, R, W), jnp.bfloat16),
            pltpu.VMEM((S - 1, 2, R, W), jnp.bfloat16),
            pltpu.VMEM((G, 5, 2, 2, 8, 128), jnp.float32),
            pltpu.VMEM((G, 2, 2, S * R, 128), jnp.float32),
            pltpu.SemaphoreType.DMA,
            pltpu.SemaphoreType.DMA,
            pltpu.SemaphoreType.DMA((2, BLOCKS)),
            pltpu.SemaphoreType.DMA((2, BLOCKS)),
            pltpu.SemaphoreType.DMA,
            pltpu.SemaphoreType.DMA((2, S)),
            pltpu.SemaphoreType.DMA((S - 1,)),
            pltpu.SemaphoreType.DMA,
            pltpu.SemaphoreType.DMA,
            pltpu.SemaphoreType.DMA,
            pltpu.SemaphoreType.DMA,
        ],
        compiler_params=pltpu.CompilerParams(collective_id=0, has_side_effects=True, vmem_limit_bytes=62_390_272),
        name="sweep",
    )(offsets, amp, phase, exit_adjoint)


def gather_kernel(other, parts, offs_ref, fwd_ref, spr_ref, grad_ref, acc):
    scan = lax.axis_index("scan")
    start = ((1 - scan) if other else scan) * (OBJ // 2)
    acc[...] = jnp.zeros_like(acc)
    lane = lax.broadcasted_iota(jnp.int32, (RUN, 128), 1)

    def per_position(position, unused):
        row_at = offs_ref[position, 0]
        col_at = offs_ref[position, 1]
        column = col_at // 128
        over = lax.rem(col_at, 128)
        keep = lane >= over
        begin = jnp.maximum(start - row_at, 0) // RUN
        end = jnp.minimum((start + OBJ // 2 - row_at + RUN - 1) // RUN, W // RUN)

        def per_run(run, unused):
            rows = pl.ds(pl.multiple_of(run * RUN, RUN), RUN)
            to = pl.ds(row_at + run * RUN - start + RUN, RUN)
            terms = [[], []]
            for j in range(2):
                cols = slice(128 * j, 128 * j + 128)
                fwd_re = fwd_ref[position, 0, rows, cols].astype(jnp.float32)
                fwd_im = fwd_ref[position, 1, rows, cols].astype(jnp.float32)
                spread = [
                    jnp.concatenate([spr_ref[position, run * (RUN // R) + i, part, :, cols] for i in range(RUN // R)], axis=0)
                    for part in range(2)
                ]
                spread_re, spread_im = (part.astype(jnp.float32) for part in spread)
                terms[0].append(pltpu.roll(fwd_re * spread_re + fwd_im * spread_im, over, 1))
                terms[1].append(pltpu.roll(fwd_re * spread_im - fwd_im * spread_re, over, 1))
            for part in parts:
                near, far = terms[part]
                part = part - parts[0]
                acc[part, column, to, :] += jnp.where(keep, near, 0.0)
                acc[part, column + 1, to, :] += jnp.where(keep, far, near)
                acc[part, column + 2, to, :] += jnp.where(keep, 0.0, far)
            return unused

        lax.fori_loop(begin, end, per_run, 0)
        return unused

    lax.fori_loop(0, G, per_position, 0)

    def split(block, unused):
        rows = pl.ds(pl.multiple_of(block * BLOCK, BLOCK), BLOCK)
        source = pl.ds(pl.multiple_of(RUN + block * BLOCK, BLOCK), BLOCK)
        for part in range(len(parts)):
            for j in range(OBJ // 128):
                grad_ref[part, rows, 128 * j : 128 * j + 128] = acc[part, j, source, :].astype(grad_ref.dtype)
        return unused

    lax.fori_loop(0, BLOCKS, split, 0)


def gather(offsets, forward, spread, other, parts):
    return pl.pallas_call(
        functools.partial(gather_kernel, other, parts),
        out_shape=jax.ShapeDtypeStruct((len(parts), OBJ // 2, OBJ), jnp.bfloat16 if other else jnp.float32),
        in_specs=[
            pl.BlockSpec(memory_space=pltpu.SMEM),
            pl.BlockSpec(memory_space=pltpu.VMEM),
            pl.BlockSpec(memory_space=pltpu.VMEM),
        ],
        out_specs=pl.BlockSpec(memory_space=pltpu.VMEM),
        scratch_shapes=[pltpu.VMEM((len(parts), OBJ // 128 + 1, OBJ // 2 + 2 * RUN, 128), jnp.float32)],
        compiler_params=pltpu.CompilerParams(vmem_limit_bytes=16 << 20),
        cost_estimate=pl.CostEstimate(flops=20_000_000, bytes_accessed=6_000_000, transcendentals=0),
        name="gather_other" if other else "gather_own",
    )(offsets, forward, spread)


def on_device(obj_amp, obj_phase, forward_waves, exit_adjoint, offsets):
    spread = sweep(offsets, obj_amp[0], obj_phase[0], exit_adjoint)
    spread = pltpu.with_memory_space_constraint(spread, pltpu.VMEM)
    forward = pltpu.with_memory_space_constraint(forward_waves[0], pltpu.VMEM)
    come = [
        lax.ppermute(gather(offsets, forward, spread, True, (part,)), "scan", [(0, 1), (1, 0)]) for part in range(2)
    ]
    keep = gather(offsets, forward, spread, False, (0, 1))
    return (keep + jnp.concatenate(come).astype(jnp.float32))[None]


def solution(mesh):
    in_specs = (
        P("sec", "scan", None),
        P("sec", "scan", None),
        P("sec", "scan", None, None, None),
        P("scan", None, None, None),
        P("scan", None),
    )
    out_specs = P("sec", None, "scan", None)
    return jax.shard_map(
        on_device, mesh=mesh, in_specs=in_specs, out_specs=out_specs, check_vma=False
    )
```

```python
import functools

import jax
import jax.numpy as jnp
from jax import lax
from jax.experimental import pallas as pl
from jax.experimental.pallas import tpu as pltpu
from jax.sharding import PartitionSpec as P

MESH = pl.DeviceIdType.MESH

damping = 0.0005
turning = 0.011

G = 8
R = 16
SKEW = 2 * G
W = 256
OBJ = 512
S = (W + SKEW) // R
TOP = 16
ROWS = OBJ + 40
AHEAD = 7
LATE = 5
COLS = OBJ + 128
FIX = 32767.0
HELD = jnp.int16
RUN = 128
BLOCK = 32
BLOCKS = OBJ // 2 // BLOCK


def behind(carry, at, value):
    top = lax.broadcasted_iota(jnp.int32, (8, 128), 0) < 1
    pieces = [carry[at]] + [value[8 * i : 8 * i + 8] for i in range(R // 8)]
    carry[at] = pieces[-1]
    rolled = [pltpu.roll(piece, 1, 0) for piece in pieces]
    return jnp.concatenate([jnp.where(top, rolled[i], rolled[i + 1]) for i in range(R // 8)], axis=0)


def times(re, im, value, j):
    return re * value[0][j] + im * value[1][j], re * value[1][j] - im * value[0][j]


def both_steps(carry, order, wave, inside, lane):
    sums, squares, here = [[], []], [[], []], [[], []]
    for part in range(2):
        v = wave[part]
        left1, left2 = ([pltpu.roll(v[j], n, 1) for j in range(2)] for n in (1, 2))
        right1, right2 = ([pltpu.roll(v[j], 128 - n, 1) for j in range(2)] for n in (1, 2))

        def pair(left, right, n):
            low, high = lane < n, lane >= 128 - n
            return [
                jnp.where(low, 0.0, left[0]) + jnp.where(high, right[1], right[0]),
                jnp.where(low, left[0], left[1]) + jnp.where(high, 0.0, right[1]),
            ]

        h = pair(left1, right1, 1)
        g = pair(left2, right2, 2)
        own = [jnp.where(lane == 0, 1.0, 2.0), jnp.where(lane == 127, 1.0, 2.0)]
        for j in range(2):
            g[j] = g[j] + own[j] * v[j]
            two = behind(carry, (order, 0, part, j), v[j])
            one = behind(carry, (order, 1, part, j), (h[j] - 4.0 * v[j]) + two)
            here[part].append(jnp.where(inside, v[j] + one, 0.0))
        sums[part] = h
        squares[part] = g
    square_re, square_im = damping * damping - turning * turning, 2.0 * damping * turning
    first_re, first_im = 2.0 * damping - 4.0 * square_re, 2.0 * turning - 4.0 * square_im
    inner = [[here[part][j] + squares[part][j] - 4.0 * sums[part][j] for j in range(2)] for part in range(2)]
    spread = [[], []]
    for j in range(2):
        last = times(square_re, square_im, here, j)
        middle = times(first_re, first_im, here, j)
        edge = times(square_re, square_im, sums, j)
        core = times(square_re, square_im, inner, j)
        for part in range(2):
            third = behind(carry, (order, 2, part, j), edge[part])
            second = behind(carry, (order, 3, part, j), (wave[part][j] + core[part]) + third)
            whole = behind(carry, (order, 4, part, j), (middle[part] + edge[part]) + second)
            spread[part].append(last[part] + whole)
    return spread


def sweep_kernel(
    offs_ref, amp_hbm, phase_hbm, exit_ref, spr_ref, amp_ref, phase_ref, half, other, padded, windows, trans, inbox, spread_out, wave_out, waves, tall,
    amp_sem, phase_sem, half_sem, half_sent, exit_sem, trans_sem, in_sem, spr_sem, trans_sent, spr_sent, wave_sent,
):
    sec = lax.axis_index("sec")
    scan = lax.axis_index("scan")
    group = sec // G
    member = lax.rem(sec, G)
    groups = lax.axis_size("sec") // G
    top = group == groups - 1

    def at(g, m):
        return (g * G + m, scan)

    loads = (
        pltpu.make_async_copy(amp_hbm, amp_ref, amp_sem),
        pltpu.make_async_copy(phase_hbm, phase_ref, phase_sem),
    )
    for load in loads:
        load.start()
    barrier = pltpu.get_barrier_semaphore()
    for step in range(1, G):
        pl.semaphore_signal(barrier, 1, device_id=at(group, lax.rem(member + step, G)), device_id_type=MESH)

    partner = (sec, 1 - scan)
    pl.semaphore_signal(barrier, 1, device_id=partner, device_id_type=MESH)

    @pl.when(group > 0)
    def _():
        pl.semaphore_signal(barrier, 1, device_id=at(group - 1, member), device_id_type=MESH)

    @pl.when(jnp.logical_not(top))
    def _():
        pl.semaphore_signal(barrier, 1, device_id=at(group + 1, member), device_id_type=MESH)

    pl.semaphore_wait(barrier, G + jnp.where(group > 0, 1, 0) + jnp.where(top, 0, 1))
    mine = G - 1 - member
    delay = 2 * (mine + 1)
    exits = pltpu.make_async_copy(exit_ref.at[member], inbox.at[:, 0:W, :], exit_sem)

    @pl.when(top)
    def _():
        exits.start()

    def block_rows(block):
        return pl.ds(pl.multiple_of(block * BLOCK, BLOCK), BLOCK)

    def chunk(part, block):
        return pltpu.make_async_remote_copy(
            src_ref=half.at[part, block_rows(block), :],
            dst_ref=other.at[part, block_rows(block), :],
            send_sem=half_sent.at[part, block],
            recv_sem=half_sem.at[part, block],
            device_id=partner,
            device_id_type=MESH,
        )

    def place(part, block, value, owner):
        to = pl.ds(pl.multiple_of(TOP + owner * (OBJ // 2) + block * BLOCK, 8), BLOCK)
        for j in range(OBJ // 128):
            padded[part, j, to, :] = value[:, 128 * j : 128 * j + 128]

    for load in loads:
        load.wait()

    for part, wave in enumerate((jnp.cos, jnp.sin)):

        def make(block, unused):
            value = amp_ref[block_rows(block), :] * wave(phase_ref[block_rows(block), :]) * FIX
            value = jnp.where(value >= 0.0, value + 0.5, value - 0.5).astype(jnp.int32)
            half[part, block_rows(block), :] = value.astype(HELD)
            chunk(part, block).start()
            place(part, block, value, scan)
            return unused

        lax.fori_loop(0, BLOCKS, make, 0)
    waves[...] = jnp.zeros_like(waves)
    inbox[:, W:, :] = jnp.zeros((2, S * R - W, W), jnp.bfloat16)
    lane = lax.broadcasted_iota(jnp.int32, (R, 128), 1)

    def take(part):
        def some_rows(block, unused):
            chunk(part, block).wait()
            place(part, block, other[part, block_rows(block), :].astype(jnp.int32), 1 - scan)
            return unused

        lax.fori_loop(0, BLOCKS, some_rows, 0)

    def give(strip, parts):
        at_row = lax.broadcasted_iota(jnp.int32, (R, 128), 0) + (strip * R - delay)
        inside = jnp.logical_and(at_row >= 0, at_row < W)
        for part in parts:
            for position in range(G):
                column = lax.shift_right_logical(offs_ref[position, 1], 7)
                over = lax.bitwise_and(offs_ref[position, 1], 127)
                turn = lax.bitwise_and(128 - over, 127)
                keep = lane < 128 - over
                rows = pl.ds(offs_ref[position, 0] + (strip * R - delay + TOP), R)
                rolled = [pltpu.roll(padded[part, column + j, rows, :], turn, 1) for j in range(3)]
                for j in range(2):
                    value = jnp.where(inside, jnp.where(keep, rolled[j], rolled[j + 1]), 0)
                    windows[part, position, strip, :, 128 * j : 128 * j + 128] = value.astype(HELD)
            trans[part, strip, mine] = windows[part, member, strip]
            for step in range(1, G):
                person = lax.rem(member + step, G)
                pltpu.make_async_remote_copy(
                    src_ref=windows.at[part, person, strip],
                    dst_ref=trans.at[part, strip, mine],
                    send_sem=trans_sent,
                    recv_sem=trans_sem.at[part, strip],
                    device_id=at(group, person),
                    device_id_type=MESH,
                ).start()

    def gives(begin, end, parts):
        def some_strips(strip, unused):
            give(strip, parts)
            return unused

        lax.fori_loop(begin, end, some_strips, 0)

    take(0)
    gives(0, AHEAD, (0,))
    take(1)
    gives(0, AHEAD, (1,))
    gives(AHEAD, S, (0, 1))

    @pl.when(top)
    def _():
        exits.wait()

    row = lax.broadcasted_iota(jnp.int32, (R, 128), 0)

    def send_spread(strip, order):
        pltpu.make_async_remote_copy(
            src_ref=spread_out.at[strip, order],
            dst_ref=spr_ref.at[member, strip],
            send_sem=spr_sent,
            recv_sem=spr_sem,
            device_id=at(group, G - 1 - order),
            device_id_type=MESH,
        ).start()

    def one_strip(strip, unused):
        @pl.when(jnp.logical_and(strip < S - 1, jnp.logical_not(top)))
        def _():
            landed = inbox.at[:, pl.ds(pl.multiple_of(strip * R, R), R), :]
            pltpu.make_async_copy(landed, landed, in_sem.at[strip]).wait()

        for part in range(2):
            come = trans.at[part, strip, 0 : G - 1]
            pltpu.make_async_copy(come, come, trans_sem.at[part, strip]).wait()
        before = jnp.maximum(strip - 1, 0)
        at_strip = pl.multiple_of(strip * R, R)
        seen = pl.multiple_of(before * R, R)
        wave = [
            [inbox[part, pl.ds(at_strip, R), 128 * j : 128 * j + 128].astype(jnp.float32) for j in range(2)]
            for part in range(2)
        ]
        for order in range(G):
            at_row = row + (strip * R - 2 * order - 1)
            inside = jnp.logical_and(at_row >= 0, at_row < W)
            spread_re, spread_im = both_steps(waves, order, wave, inside, lane)
            wave = [[], []]
            for j in range(2):
                cols = slice(128 * j, 128 * j + 128)
                tall[order, 0, j, pl.ds(at_strip, R), :] = spread_re[j]
                tall[order, 1, j, pl.ds(at_strip, R), :] = spread_im[j]
                win_re = trans[0, strip, order, :, cols].astype(jnp.int32).astype(jnp.float32)
                win_im = trans[1, strip, order, :, cols].astype(jnp.int32).astype(jnp.float32)
                out_re = ((win_re * spread_re[j] + win_im * spread_im[j]) * (1.0 / FIX)).astype(jnp.bfloat16)
                out_im = ((win_re * spread_im[j] - win_im * spread_re[j]) * (1.0 / FIX)).astype(jnp.bfloat16)
                if order < G - 1:
                    wave[0].append(out_re.astype(jnp.float32))
                    wave[1].append(out_im.astype(jnp.float32))
                else:
                    wave_out[before, 0, :, cols] = out_re
                    wave_out[before, 1, :, cols] = out_im

        @pl.when(jnp.logical_and(strip > 0, group > 0))
        def _():
            pltpu.make_async_remote_copy(
                src_ref=wave_out.at[strip - 1],
                dst_ref=inbox.at[:, pl.ds(seen, R), :],
                send_sem=wave_sent,
                recv_sem=in_sem.at[strip - 1],
                device_id=at(group - 1, member),
                device_id_type=MESH,
            ).start()

        @pl.when(strip > 0)
        def _():
            for order in range(G):
                lag = 2 * (order + 1)
                for part in range(2):
                    for j in range(2):
                        spread_out[before, order, part, :, 128 * j : 128 * j + 128] = tall[
                            order, part, j, pl.ds(seen + lag, R), :
                        ].astype(jnp.bfloat16)

                @pl.when(jnp.logical_and(group < LATE, member != G - 1 - order))
                def _():
                    send_spread(strip - 1, order)

        @pl.when(strip > 0)
        def _():
            spr_ref[member, strip - 1] = spread_out[strip - 1, mine]

        return unused

    lax.fori_loop(0, S, one_strip, 0)

    @pl.when(group >= LATE)
    def _():
        def rest(strip, unused):
            for order in range(G):

                @pl.when(member != G - 1 - order)
                def _():
                    send_spread(strip, order)

            return unused

        lax.fori_loop(0, S - 1, rest, 0)

    pltpu.make_async_copy(windows.at[:, 0 : G - 1], windows.at[:, 0 : G - 1], trans_sent).wait()
    pltpu.make_async_copy(spr_ref.at[0 : G - 1], spr_ref.at[0 : G - 1], spr_sent).wait()

    @pl.when(group > 0)
    def _():
        pltpu.make_async_copy(wave_out, wave_out, wave_sent).wait()

    pltpu.make_async_copy(spr_ref.at[0 : G - 1], spr_ref.at[0 : G - 1], spr_sem).wait()


def sweep(offsets, amp, phase, exit_adjoint):
    return pl.pallas_call(
        sweep_kernel,
        out_shape=pltpu.VMEM((G, S - 1, 2, R, W), jnp.bfloat16),
        in_specs=[
            pl.BlockSpec(memory_space=pltpu.SMEM),
            pl.BlockSpec(memory_space=pl.ANY),
            pl.BlockSpec(memory_space=pl.ANY),
            pl.BlockSpec(memory_space=pl.ANY),
        ],
        out_specs=pl.BlockSpec(memory_space=pltpu.VMEM),
        scratch_shapes=[
            pltpu.VMEM((OBJ // 2, OBJ), jnp.float32),
            pltpu.VMEM((OBJ // 2, OBJ), jnp.float32),
            pltpu.VMEM((2, OBJ // 2, OBJ), HELD),
            pltpu.VMEM((2, OBJ // 2, OBJ), HELD),
            pltpu.VMEM((2, OBJ // 128 + 1, ROWS, 128), jnp.int32),
            pltpu.VMEM((2, G, S, R, W), HELD),
            pltpu.VMEM((2, S, G, R, W), HELD),
            pltpu.VMEM((2, S * R, W), jnp.bfloat16),
            pltpu.VMEM((S - 1, G, 2, R, W), jnp.bfloat16),
            pltpu.VMEM((S - 1, 2, R, W), jnp.bfloat16),
            pltpu.VMEM((G, 5, 2, 2, 8, 128), jnp.float32),
            pltpu.VMEM((G, 2, 2, S * R, 128), jnp.float32),
            pltpu.SemaphoreType.DMA,
            pltpu.SemaphoreType.DMA,
            pltpu.SemaphoreType.DMA((2, BLOCKS)),
            pltpu.SemaphoreType.DMA((2, BLOCKS)),
            pltpu.SemaphoreType.DMA,
            pltpu.SemaphoreType.DMA((2, S)),
            pltpu.SemaphoreType.DMA((S - 1,)),
            pltpu.SemaphoreType.DMA,
            pltpu.SemaphoreType.DMA,
            pltpu.SemaphoreType.DMA,
            pltpu.SemaphoreType.DMA,
        ],
        compiler_params=pltpu.CompilerParams(collective_id=0, has_side_effects=True, vmem_limit_bytes=62_390_272),
        name="sweep",
    )(offsets, amp, phase, exit_adjoint)


def gather_kernel(other, parts, offs_ref, fwd_ref, spr_ref, grad_ref, acc):
    scan = lax.axis_index("scan")
    start = ((1 - scan) if other else scan) * (OBJ // 2)
    acc[...] = jnp.zeros_like(acc)
    lane = lax.broadcasted_iota(jnp.int32, (RUN, 128), 1)

    def per_position(position, unused):
        row_at = offs_ref[position, 0]
        col_at = offs_ref[position, 1]
        column = col_at // 128
        over = lax.rem(col_at, 128)
        keep = lane >= over
        begin = jnp.maximum(start - row_at, 0) // RUN
        end = jnp.minimum((start + OBJ // 2 - row_at + RUN - 1) // RUN, W // RUN)

        def per_run(run, unused):
            rows = pl.ds(pl.multiple_of(run * RUN, RUN), RUN)
            to = pl.ds(row_at + run * RUN - start + RUN, RUN)
            terms = [[], []]
            for j in range(2):
                cols = slice(128 * j, 128 * j + 128)
                fwd_re = fwd_ref[position, 0, rows, cols].astype(jnp.float32)
                fwd_im = fwd_ref[position, 1, rows, cols].astype(jnp.float32)
                spread = [
                    jnp.concatenate([spr_ref[position, run * (RUN // R) + i, part, :, cols] for i in range(RUN // R)], axis=0)
                    for part in range(2)
                ]
                spread_re, spread_im = (part.astype(jnp.float32) for part in spread)
                terms[0].append(pltpu.roll(fwd_re * spread_re + fwd_im * spread_im, over, 1))
                terms[1].append(pltpu.roll(fwd_re * spread_im - fwd_im * spread_re, over, 1))
            for part in parts:
                near, far = terms[part]
                part = part - parts[0]
                acc[part, column, to, :] += jnp.where(keep, near, 0.0)
                acc[part, column + 1, to, :] += jnp.where(keep, far, near)
                acc[part, column + 2, to, :] += jnp.where(keep, 0.0, far)
            return unused

        lax.fori_loop(begin, end, per_run, 0)
        return unused

    lax.fori_loop(0, G, per_position, 0)

    def split(block, unused):
        rows = pl.ds(pl.multiple_of(block * BLOCK, BLOCK), BLOCK)
        source = pl.ds(pl.multiple_of(RUN + block * BLOCK, BLOCK), BLOCK)
        for part in range(len(parts)):
            for j in range(OBJ // 128):
                grad_ref[part, rows, 128 * j : 128 * j + 128] = acc[part, j, source, :].astype(grad_ref.dtype)
        return unused

    lax.fori_loop(0, BLOCKS, split, 0)


def gather(offsets, forward, spread, other, parts):
    return pl.pallas_call(
        functools.partial(gather_kernel, other, parts),
        out_shape=jax.ShapeDtypeStruct((len(parts), OBJ // 2, OBJ), jnp.bfloat16 if other else jnp.float32),
        in_specs=[
            pl.BlockSpec(memory_space=pltpu.SMEM),
            pl.BlockSpec(memory_space=pltpu.VMEM),
            pl.BlockSpec(memory_space=pltpu.VMEM),
        ],
        out_specs=pl.BlockSpec(memory_space=pltpu.VMEM),
        scratch_shapes=[pltpu.VMEM((len(parts), OBJ // 128 + 1, OBJ // 2 + 2 * RUN, 128), jnp.float32)],
        compiler_params=pltpu.CompilerParams(vmem_limit_bytes=16 << 20),
        cost_estimate=pl.CostEstimate(flops=20_000_000, bytes_accessed=6_000_000, transcendentals=0),
        name="gather_other" if other else "gather_own",
    )(offsets, forward, spread)


def on_device(obj_amp, obj_phase, forward_waves, exit_adjoint, offsets):
    spread = sweep(offsets, obj_amp[0], obj_phase[0], exit_adjoint)
    spread = pltpu.with_memory_space_constraint(spread, pltpu.VMEM)
    forward = pltpu.with_memory_space_constraint(forward_waves[0], pltpu.VMEM)
    come = [
        lax.ppermute(gather(offsets, forward, spread, True, (part,)), "scan", [(0, 1), (1, 0)]) for part in range(2)
    ]
    keep = gather(offsets, forward, spread, False, (0, 1))
    return (keep + jnp.concatenate(come).astype(jnp.float32))[None]


def solution(mesh):
    in_specs = (
        P("sec", "scan", None),
        P("sec", "scan", None),
        P("sec", "scan", None, None, None),
        P("scan", None, None, None),
        P("scan", None),
    )
    out_specs = P("sec", None, "scan", None)
    return jax.shard_map(
        on_device, mesh=mesh, in_specs=in_specs, out_specs=out_specs, check_vma=False
    )
```
